32 devices in a mesh: dp: 4 (over y, x), seq: 8 (over z, core).
Axes of the slice: x: 2, y: 2, z: 4, core: 2. Of those that a mesh axis runs over, the one named last changes fastest.
Arguments:
- tokens: bfloat16 [4, 8192, 1152], P('dp', 'seq'), may hold values from -40 to 40
- d_out: bfloat16 [4, 8192, 1152], P('dp', 'seq'), may hold values from -6 to 6
- frames: int32 [4], P('dp'), may hold values from 16 to 32, as said below
- frame_order: int32 [4, 32], P('dp'), may hold values from 0 to 31, each once within a row
- w_qkv: bfloat16 [1152, 3456], replicated, may hold values from -4 to 4
- w_out: bfloat16 [1152, 1152], replicated, may hold values from -0.1875 to 0.1875
Outputs:
- d_tokens: bfloat16 [4, 8192, 1152], P('dp', 'seq')
- d_w_out: float32 [1152, 1152], P('seq', 'dp')
The draws below stay inside these ranges and needn't reach their ends.
Inputs may be any that keep to these rules, and one draw needn't show every extreme that they name: Some clip has 32 frames. `frame_order`: each row holds every number of 0 to 31 once.
All inputs are finite; a program needn't handle non-finite values.
Results may differ from the reference program's by a relative error of at most 0.012.
The reference program's roundings to bfloat16 on the way count: a program that leaves them out, or rounds other values in their place, can miss the bound.
Values may be sent and summed in bfloat16 or wider, within the bound.
A program may use at most 128 MiB of HBM per device.

```python
import math
import jax
import jax.numpy as jnp
from jax import lax

D = 1152
H = 16
P_SIZE = 256
F_MAX = 32
CLIPS = 1
CLIP_TOTAL = 4
ROWS = 8192
N_DP = 4


def draw_frames(key, part):
    clip_total = N_DP * CLIPS
    counts = jax.random.randint(jax.random.fold_in(key, 11), (clip_total,), F_MAX // 2, F_MAX + 1)
    largest_at = jax.random.randint(jax.random.fold_in(key, 12), (), 0, clip_total)
    return jnp.where(jnp.arange(clip_total) == largest_at, F_MAX, counts).astype(jnp.int32)


def draw_tokens(key, part):
    full_shape = (N_DP * CLIPS, F_MAX, P_SIZE, D)
    row_scales = jnp.exp(jax.random.uniform(jax.random.fold_in(key, 21), (N_DP * CLIPS, F_MAX, P_SIZE, 1), jnp.float32) * jnp.log(10.0))
    gaussian = jnp.clip(jax.random.normal(jax.random.fold_in(key, 23), full_shape, jnp.float32), -4.0, 4.0)
    result = gaussian * row_scales
    return result.reshape(N_DP * CLIPS, F_MAX * P_SIZE, D).astype(jnp.bfloat16)


def draw_w_qkv(key, part):
    matrix = jnp.clip(jax.random.normal(jax.random.fold_in(key, 31), (D, 3 * D), jnp.float32), -4.0, 4.0) * D ** (-0.5)
    return jnp.clip(matrix, -4.0, 4.0).astype(jnp.bfloat16)


def with_spikes(drawn, key, source, target, blocks, factor):
    owner, partner = [(jnp.arange(drawn.shape[dim]) // (drawn.shape[dim] // blocks)).reshape([-1 if axis == dim else 1 for axis in range(drawn.ndim)]) for dim in (source, target)]
    chosen = jax.random.permutation(key, blocks)[partner]
    strong = (owner == chosen) | (owner == (partner + blocks // 2) % blocks)
    return jnp.where(strong, factor * drawn, drawn)


def block_scale(stream_key, extent, shards, least, top_value):
    loudness = 1.0
    for axis_at, shards_of in shards:
        draws = jax.random.uniform(jax.random.fold_in(jax.random.fold_in(stream_key, 6), axis_at), (shards_of,), jnp.float32, least / len(shards), top_value / len(shards))
        loudness = loudness * jnp.repeat(jnp.exp(draws), extent[axis_at] // shards_of).reshape((-1,) + (1,) * (len(extent) - 1 - axis_at))
    return loudness


def bell_draw(own_key, dims, width, bound, split=(), held_as=jnp.bfloat16):
    entries = jax.random.normal(own_key, dims, jnp.float32) * width
    if len(split) > 0:
        entries = block_scale(own_key, dims, split, -0.22, 0.18) * entries
    return jnp.clip(entries, min=-bound, max=bound).astype(held_as)


def heavy_noise(key, dims, scale, reach, cuts, heavy, dtype=jnp.bfloat16):
    entries = scale * jax.random.normal(key, dims, jnp.float32)
    if cuts:
        entries = entries * block_scale(key, dims, cuts, -0.22, 0.18)
    return jnp.clip(with_spikes(entries, jax.random.fold_in(key, 3), *heavy), -reach, reach).astype(dtype)


def setup_inputs(seed: int = 0) -> dict:
    key_of = jax.random.split(jax.random.key(seed), 7)
    tokens = draw_tokens(jax.random.fold_in(key_of[6], 71), 0)
    d_out = heavy_noise(key_of[1], (CLIP_TOTAL, ROWS, D), 1.0, 6.0, ((0, 4), (1, 8)), (1, 2, 8, 2.0))
    frames = draw_frames(jax.random.fold_in(key_of[6], 71), 0)
    frame_order = jax.vmap(lambda own: jax.random.permutation(own, F_MAX))(jax.random.split(key_of[3], CLIP_TOTAL)).reshape((CLIP_TOTAL, F_MAX)).astype(jnp.int32)
    w_qkv = draw_w_qkv(jax.random.fold_in(key_of[6], 71), 0)
    w_out = bell_draw(key_of[5], (D, D), D ** -0.5, 0.1875)
    return dict(tokens=tokens, d_out=d_out, frames=frames, frame_order=frame_order, w_qkv=w_qkv, w_out=w_out)


def layer_stats(tokens):
    values = tokens.astype(jnp.float32)
    center = values - lax.optimization_barrier(jnp.mean(values, axis=-1, keepdims=True))
    spread = lax.optimization_barrier(jnp.mean(center * center, axis=-1, keepdims=True))
    inverse = lax.rsqrt(spread + 1e-06)
    return (center * inverse, inverse)

def attend_forward(queries, keys_in, values, live_slots, score_scale):
    scores = jnp.einsum('ciqhe,cjqhe->cqhij', queries.astype(jnp.float32), keys_in.astype(jnp.float32)) * score_scale
    scores = jnp.where(live_slots[:, None, None, None, :] > 0.5, scores, -1e+30)
    row_max = lax.optimization_barrier(jnp.max(scores, axis=-1, keepdims=True))
    exponent = jnp.exp(scores - row_max)
    softmax_out = exponent / lax.optimization_barrier(jnp.sum(exponent, axis=-1, keepdims=True))
    rounded = softmax_out.astype(jnp.bfloat16)
    attended = jnp.einsum('cqhij,cjqhe->ciqhe', rounded.astype(jnp.float32), values.astype(jnp.float32)).astype(jnp.bfloat16)
    return (softmax_out, rounded, attended)

def attend_backward(queries, keys_in, values, softmax_out, rounded, head_grad, score_scale):
    grad_float = head_grad.astype(jnp.float32)
    d_values = jnp.einsum('cqhij,ciqhe->cjqhe', rounded.astype(jnp.float32), grad_float).astype(jnp.bfloat16)
    prob_grad = jnp.einsum('ciqhe,cjqhe->cqhij', grad_float, values.astype(jnp.float32))
    inner_sum = lax.optimization_barrier(jnp.sum(softmax_out * prob_grad, axis=-1, keepdims=True))
    score_grad = (softmax_out * (prob_grad - inner_sum) * score_scale).astype(jnp.bfloat16)
    score_float = score_grad.astype(jnp.float32)
    d_queries = jnp.einsum('cqhij,cjqhe->ciqhe', score_float, keys_in.astype(jnp.float32)).astype(jnp.bfloat16)
    d_keys = jnp.einsum('cqhij,ciqhe->cjqhe', score_float, queries.astype(jnp.float32)).astype(jnp.bfloat16)
    return (d_queries, d_keys, d_values)

def reference(tokens, d_out, frames, frame_order, w_qkv, w_out):
    head_dim = D // H
    score_scale = 1.0 / math.sqrt(head_dim)
    grad_out = jnp.zeros((D, D), jnp.float32)
    results = []
    for clip_index in range(N_DP * CLIPS):
        live_slots = (frame_order[clip_index] < frames[clip_index]).astype(jnp.float32)
        row_live = jnp.repeat(live_slots, P_SIZE)
        normalized, inverse = layer_stats(tokens[clip_index])
        normed = normalized.astype(jnp.bfloat16)
        joined = jnp.dot(normed, w_qkv, preferred_element_type=jnp.float32).astype(jnp.bfloat16)
        head_grid = joined.reshape(1, F_MAX, P_SIZE, 3, H, head_dim)
        queries = head_grid[:, :, :, 0]
        keys_in = head_grid[:, :, :, 1]
        values = head_grid[:, :, :, 2]
        softmax_out, rounded, attended = attend_forward(queries, keys_in, values, live_slots[None, :], score_scale)
        masked = (d_out[clip_index].astype(jnp.float32) * row_live[:, None]).astype(jnp.bfloat16)
        head_rows = jnp.dot(masked, w_out.T, preferred_element_type=jnp.float32).astype(jnp.bfloat16)
        attended_rows = attended.reshape(F_MAX * P_SIZE, D)
        grad_out = grad_out + jnp.dot(attended_rows.T, masked, preferred_element_type=jnp.float32)
        head_grad = head_rows.reshape(1, F_MAX, P_SIZE, H, head_dim)
        d_queries, d_keys, d_values = attend_backward(queries, keys_in, values, softmax_out, rounded, head_grad, score_scale)
        qkv_grad = jnp.stack((d_queries, d_keys, d_values), axis=3).reshape(F_MAX * P_SIZE, 3 * D)
        normed_grad = jnp.dot(qkv_grad, w_qkv.T, preferred_element_type=jnp.float32)
        mean_grad = lax.optimization_barrier(jnp.mean(normed_grad, axis=-1, keepdims=True))
        mean_cross = lax.optimization_barrier(jnp.mean(normed_grad * normalized, axis=-1, keepdims=True))
        d_rows = masked.astype(jnp.float32) + inverse * (normed_grad - mean_grad - normalized * mean_cross)
        results.append(d_rows.astype(jnp.bfloat16))
    return (jnp.stack(results, axis=0), grad_out)
```

```python
import functools
import math

import jax
import jax.numpy as jnp
from jax import lax
from jax.experimental import pallas as pl
from jax.experimental.pallas import tpu as pltpu
from jax.sharding import PartitionSpec as P

H = 16
LANES = 128
GROUP = 8
AHEAD = 3
HOLD = 1
NT = (((1,), (1,)), ((), ()))
TN = (((0,), (0,)), ((), ()))


def dot(a, b, dims=(((1,), (0,)), ((), ()))):
    return lax.dot_general(a, b, dims, preferred_element_type=jnp.float32)


def attend(joined, head_grad, mask, attended, qkv_grad, width, score_scale):
    head_dim = width // H
    column = lax.broadcasted_iota(jnp.int32, (1, 2 * LANES), 1)
    pending = [{}, {}, {}, {}]
    for h in range(H):
        low, high = h * head_dim, (h + 1) * head_dim
        first, last = low // LANES, -(-high // LANES)
        start, size = first * LANES, (last - first) * LANES
        keep = jnp.where(
            (column[:, :size] >= low - start) & (column[:, :size] < high - start), 1.0, 0.0
        ).astype(jnp.bfloat16)
        q = joined[:, start : start + size] * keep
        k = joined[:, width + start : width + start + size] * keep
        v = joined[:, 2 * width + start : 2 * width + start + size] * keep
        g = head_grad[:, start : start + size] * keep
        scores = dot(q, k, NT) * score_scale + mask
        exponent = jnp.exp(scores - jnp.max(scores, axis=-1, keepdims=True))
        probs = exponent * (1.0 / jnp.sum(exponent, axis=-1, keepdims=True))
        rounded = probs.astype(jnp.bfloat16)
        prob_grad = dot(g, v, NT)
        inner = jnp.sum(probs * prob_grad, axis=-1, keepdims=True)
        score_grad = (probs * (prob_grad - inner) * score_scale).astype(jnp.bfloat16)
        results = (
            dot(rounded, v),
            dot(score_grad, k),
            dot(score_grad, q, TN),
            dot(rounded, g, TN),
        )
        for which, result in enumerate(results):
            for tile in range(first, last):
                piece = result[:, (tile - first) * LANES : (tile - first + 1) * LANES]
                held = pending[which].pop(tile, None)
                piece = piece if held is None else held + piece
                if (tile + 1) * LANES <= high:
                    piece = piece.astype(jnp.bfloat16)
                    if which == 0:
                        attended[:, tile * LANES : (tile + 1) * LANES] = piece
                    else:
                        at = (which - 1) * width + tile * LANES
                        qkv_grad[:, at : at + LANES] = piece
                else:
                    pending[which][tile] = piece


def kernel(
    score_scale,
    tokens_ref,
    d_out_ref,
    live_ref,
    mask_ref,
    w_qkv_ref,
    w_out_ref,
    d_tokens_ref,
    grad_ref,
    joined,
    head_grad,
    attended,
    qkv_grad,
):
    rows, width = attended.shape
    values = tokens_ref[...].astype(jnp.float32).reshape(rows, width)
    center = values - jnp.mean(values, axis=-1, keepdims=True)
    inverse = lax.rsqrt(jnp.mean(center * center, axis=-1, keepdims=True) + 1e-06)
    normalized = center * inverse
    normed = normalized.astype(jnp.bfloat16)
    masked_wide = d_out_ref[...].astype(jnp.float32).reshape(rows, width) * live_ref[...]
    masked = masked_wide.astype(jnp.bfloat16)
    joined[...] = dot(normed, w_qkv_ref[...]).astype(jnp.bfloat16)
    head_grad[...] = dot(masked, w_out_ref[...], NT).astype(jnp.bfloat16)
    attend(joined, head_grad, mask_ref[...], attended, qkv_grad, width, score_scale)
    term = dot(attended[...], masked, TN)

    @pl.when(pl.program_id(0) == 0)
    def _():
        grad_ref[...] = term

    @pl.when(pl.program_id(0) != 0)
    def _():
        grad_ref[...] += term

    normed_grad = dot(qkv_grad[...], w_qkv_ref[...], NT)
    mean_grad = jnp.mean(normed_grad, axis=-1, keepdims=True)
    mean_cross = jnp.mean(normed_grad * normalized, axis=-1, keepdims=True)
    result = masked_wide + inverse * (normed_grad - mean_grad - normalized * mean_cross)
    d_tokens_ref[...] = result.reshape(d_tokens_ref.shape).astype(jnp.bfloat16)


def mask_of(live_slots, rows, group):
    at = jnp.arange(rows, dtype=jnp.int32)
    live_rows = jnp.repeat(live_slots, group)
    mask = jnp.where(
        (at[:, None] % group == at[None, :] % group) & (live_rows[None, :] > 0.5), 0.0, -1e30
    ).astype(jnp.float32)
    return live_rows, mask


def local_part(tokens, d_out, live_slots, w_qkv, w_out):
    slot_count, stripe, width = tokens.shape
    group = min(GROUP, stripe)
    rows = slot_count * group
    steps = stripe // group
    live_rows, mask = mask_of(live_slots, rows, group)
    if steps == 1:
        tokens, d_out = tokens.reshape(rows, width), d_out.reshape(rows, width)
        moving = pl.BlockSpec((rows, width), lambda i: (0, 0))
    else:
        moving = pl.BlockSpec((slot_count, group, width), lambda i: (0, i, 0))

    def whole(shape):
        return pl.BlockSpec(shape, lambda i: (0, 0), pipeline_mode=pl.Buffered(1))

    d_tokens, grad = pl.pallas_call(
        functools.partial(kernel, 1.0 / math.sqrt(width // H)),
        grid=(steps,),
        in_specs=[
            moving,
            moving,
            whole((rows, 1)),
            whole((rows, rows)),
            whole(w_qkv.shape),
            whole(w_out.shape),
        ],
        out_specs=[moving, whole((width, width))],
        out_shape=[
            jax.ShapeDtypeStruct(tokens.shape, jnp.bfloat16),
            jax.ShapeDtypeStruct((width, width), jnp.float32),
        ],
        scratch_shapes=[
            pltpu.VMEM((rows, 3 * width), jnp.bfloat16),
            pltpu.VMEM((rows, width), jnp.bfloat16),
            pltpu.VMEM((rows, width), jnp.bfloat16),
            pltpu.VMEM((rows, 3 * width), jnp.bfloat16),
        ],
        compiler_params=pltpu.CompilerParams(
            dimension_semantics=("arbitrary",), vmem_limit_bytes=60 * 2**20
        ),
    )(tokens, d_out, live_rows[:, None], mask, w_qkv, w_out)
    return d_tokens.reshape(slot_count, stripe, width), grad


def mask_in_kernel(group, order, count):
    rows = order.shape[1] * group
    live = (order < count).astype(jnp.float32)
    slot_of = lax.broadcasted_iota(jnp.int32, (rows, order.shape[1]), 1) * group
    row_of = lax.broadcasted_iota(jnp.int32, slot_of.shape, 0)
    owns = (row_of >= slot_of) & (row_of < slot_of + group)
    live_rows = jnp.sum(jnp.where(owns, live, 0.0), axis=-1, keepdims=True)
    live_columns = dot(jnp.broadcast_to(live, (8, order.shape[1])), owns.astype(jnp.float32), NT)
    row = lax.broadcasted_iota(jnp.int32, (rows, rows), 0)
    column = lax.broadcasted_iota(jnp.int32, (rows, rows), 1)
    same = lax.rem(row, group) == lax.rem(column, group)
    mask = jnp.where(same & (live_columns[:1] > 0.5), 0.0, -1e30)
    return live_rows, mask


def head_window(width, h):
    head_dim = width // H
    low, high = h * head_dim, (h + 1) * head_dim
    first, last = low // LANES, -(-high // LANES)
    start, size = first * LANES, (last - first) * LANES
    column = lax.broadcasted_iota(jnp.int32, (1, 2 * LANES), 1)
    keep = jnp.where(
        (column[:, :size] >= low - start) & (column[:, :size] < high - start), 1.0, 0.0
    ).astype(jnp.bfloat16)
    return start, size, high, keep


def put_head(pending, result, start, size, high, target, offset):
    for tile in range(start // LANES, (start + size) // LANES):
        piece = result[:, tile * LANES - start : (tile + 1) * LANES - start]
        held = pending.pop(tile, None)
        piece = piece if held is None else held + piece
        if (tile + 1) * LANES <= high:
            at = offset + tile * LANES
            target[:, at : at + LANES] = piece.astype(jnp.bfloat16)
        else:
            pending[tile] = piece


def attend_forward(joined, mask, attended, probs_ref, width, score_scale):
    pending = {}
    for h in range(H):
        start, size, high, keep = head_window(width, h)
        q = joined[:, start : start + size] * keep
        k = joined[:, width + start : width + start + size]
        v = joined[:, 2 * width + start : 2 * width + start + size] * keep
        scores = dot(q, k, NT) * score_scale + mask
        exponent = jnp.exp(scores - jnp.max(scores, axis=-1, keepdims=True))
        probs = exponent * (1.0 / jnp.sum(exponent, axis=-1, keepdims=True))
        probs_ref[h] = probs
        result = dot(probs.astype(jnp.bfloat16), v)
        put_head(pending, result, start, size, high, attended, 0)


def attend_backward(joined, head_grad, probs_ref, qkv_grad, width, score_scale):
    pending = [{}, {}, {}]
    for h in range(H):
        start, size, high, keep = head_window(width, h)
        q = joined[:, start : start + size] * keep
        k = joined[:, width + start : width + start + size] * keep
        v = joined[:, 2 * width + start : 2 * width + start + size]
        g = head_grad[:, start : start + size] * keep
        probs = probs_ref[h]
        prob_grad = dot(g, v, NT)
        inner = jnp.sum(probs * prob_grad, axis=-1, keepdims=True)
        score_grad = (probs * (prob_grad - inner) * score_scale).astype(jnp.bfloat16)
        results = (
            dot(score_grad, k),
            dot(score_grad, q, TN),
            dot(probs.astype(jnp.bfloat16), g, TN),
        )
        for which, result in enumerate(results):
            put_head(pending[which], result, start, size, high, qkv_grad, which * width)


def exchange_kernel(
    score_scale,
    seq_size,
    dp_size,
    tokens_ref,
    d_out_ref,
    count_ref,
    order_ref,
    w_qkv_hbm,
    w_out_hbm,
    d_tokens_ref,
    final_ref,
    w_qkv_ref,
    w_out_ref,
    got_tokens,
    got_d_out,
    results,
    joined,
    head_grad,
    attended,
    qkv_grad,
    grad,
    probs_ref,
    live_ref,
    mask_ref,
    pair_sent,
    pair_got,
    dp_sent,
    dp_got,
    held,
    chip_sent,
    chip_got,
    weight_sems,
    tokens_send,
    tokens_recv,
    d_out_send,
    d_out_recv,
    back_send,
    back_recv,
    pair_sems,
    dp_send,
    dp_recv,
    chip_send,
    chip_recv,
):
    rows, width = attended.shape
    steps, slot_count, group, _ = got_tokens.shape
    slots = tokens_ref.shape[0]
    stripe = steps * group
    chips = seq_size // 2
    row_block, column_block = final_ref.shape
    me = lax.axis_index("seq")
    my_dp = lax.axis_index("dp")
    core = lax.rem(me, 2)
    chip = me // 2
    far_first = tuple(reversed(range(1, seq_size)))

    def peer(k):
        return me ^ k

    def dp_peer(k):
        return lax.rem(my_dp + k, dp_size)

    barrier = pltpu.get_barrier_semaphore()
    for k in range(1, seq_size):
        pl.semaphore_signal(
            barrier,
            inc=1,
            device_id={"seq": peer(k)},
            device_id_type=pl.DeviceIdType.MESH,
        )
    for k in range(1, dp_size):
        pl.semaphore_signal(
            barrier,
            inc=1,
            device_id={"dp": dp_peer(k)},
            device_id_type=pl.DeviceIdType.MESH,
        )
    pl.semaphore_wait(barrier, seq_size - 1 + dp_size - 1)

    def remote(source, target, send, recv, device):
        return pltpu.make_async_remote_copy(
            src_ref=source,
            dst_ref=target,
            send_sem=send,
            recv_sem=recv,
            device_id=device,
            device_id_type=pl.DeviceIdType.MESH,
        )

    def home(ref, owner, g):
        return ref.at[:, pl.ds(pl.multiple_of(owner * stripe + g * group, group), group), :]

    def away(ref, owner, g):
        return ref.at[g, pl.ds(owner * slots, slots)]

    def spread(source, target, send, recv, g, k):
        return remote(
            home(source, peer(k), g),
            away(target, me, g),
            send.at[g, k],
            recv.at[g, k],
            {"seq": peer(k)},
        )

    def keep_own(source, target, recv, g):
        return pltpu.make_async_copy(home(source, me, g), away(target, me, g), recv.at[g, 0])

    def back(g, k):
        return remote(
            away(results, peer(k), g),
            home(d_tokens_ref, me, g),
            back_send.at[g, k],
            back_recv.at[g, k],
            {"seq": peer(k)},
        )

    def back_own(g):
        return pltpu.make_async_copy(
            away(results, me, g), home(d_tokens_ref, me, g), back_recv.at[g, 0]
        )

    moved = (
        (tokens_ref, got_tokens, tokens_send, tokens_recv),
        (d_out_ref, got_d_out, d_out_send, d_out_recv),
    )

    def depart(which, g):
        source, target, send, recv = moved[which]
        for k in far_first:
            spread(source, target, send, recv, g, k).start()
        keep_own(source, target, recv, g).start()

    def arrived(which, g):
        source, target, send, recv = moved[which]
        for k in far_first:
            spread(source, target, send, recv, g, k).wait_recv()
        keep_own(source, target, recv, g).wait()

    def give_back(g):
        for k in far_first:
            back(g, k).start()
        back_own(g).start()

    for at in range(min(AHEAD, 2 * steps)):
        depart(at % 2, at // 2)
    weights = (
        pltpu.make_async_copy(w_qkv_hbm, w_qkv_ref, weight_sems.at[0]),
        pltpu.make_async_copy(w_out_hbm, w_out_ref, weight_sems.at[1]),
    )
    for copy in weights:
        copy.start()
    live_ref[...], mask_ref[...] = mask_in_kernel(group, order_ref[...], count_ref[0])
    grad[...] = jnp.zeros_like(grad)
    for copy in weights:
        copy.wait()

    def depart_next(which, g):
        at = AHEAD + which
        later = g + at // 2

        @pl.when(later < steps)
        def _():
            depart(at % 2, later)

    def pair_copy():
        return remote(
            pair_sent, pair_got, pair_sems.at[0], pair_sems.at[1], {"seq": chip * 2 + 1 - core}
        )

    def row_piece(at, parity):
        start = pl.multiple_of((at * 2 + parity) * row_block, row_block)
        return grad[pl.ds(start, row_block), :]

    def columns_of(value, d):
        return value[:, d * column_block : (d + 1) * column_block]

    def dp_copy(k):
        return remote(
            dp_sent.at[dp_peer(k)],
            dp_got.at[k - 1],
            dp_send.at[k - 1],
            dp_recv.at[k - 1],
            {"dp": dp_peer(k)},
        )

    @pl.loop(0, steps)
    def _(g):
        arrived(0, g)
        depart_next(0, g)
        values = got_tokens[g].astype(jnp.float32).reshape(rows, width)
        center = values - jnp.mean(values, axis=-1, keepdims=True)
        inverse = lax.rsqrt(jnp.mean(center * center, axis=-1, keepdims=True) + 1e-06)
        normalized = center * inverse
        joined[...] = dot(normalized.astype(jnp.bfloat16), w_qkv_ref[...]).astype(jnp.bfloat16)
        attend_forward(joined, mask_ref[...], attended, probs_ref, width, score_scale)
        arrived(1, g)
        depart_next(1, g)
        masked_wide = got_d_out[g].astype(jnp.float32).reshape(rows, width) * live_ref[...]
        masked = masked_wide.astype(jnp.bfloat16)
        grad[...] += dot(attended[...], masked, TN)

        @pl.when(g == steps - 1)
        def _():
            @pl.loop(0, chips)
            def _(at):
                value = row_piece(at, 1 - core)
                for d in range(dp_size):
                    pair_sent[d, at] = columns_of(value, d).astype(jnp.bfloat16)

            pair_copy().start()

        head_grad[...] = dot(masked, w_out_ref[...], NT).astype(jnp.bfloat16)

        @pl.when(g == steps - 1)
        def _():
            pair_copy().wait_recv()

            @pl.loop(0, chips)
            def _(at):
                value = row_piece(at, core)
                for d in range(dp_size):
                    total = columns_of(value, d) + pair_got[d, at].astype(jnp.float32)
                    dp_sent[d, at] = total.astype(jnp.bfloat16)

            for k in range(1, dp_size):
                dp_copy(k).start()

        @pl.when(g > HOLD)
        def _():
            give_back(g - 1 - HOLD)

        attend_backward(joined, head_grad, probs_ref, qkv_grad, width, score_scale)
        normed_grad = dot(qkv_grad[...], w_qkv_ref[...], NT)
        mean_grad = jnp.mean(normed_grad, axis=-1, keepdims=True)
        mean_cross = jnp.mean(normed_grad * normalized, axis=-1, keepdims=True)
        result = masked_wide + inverse * (normed_grad - mean_grad - normalized * mean_cross)
        results[g] = result.reshape(slot_count, group, width).astype(jnp.bfloat16)

    for g in range(max(0, steps - 1 - HOLD), steps):
        give_back(g)
    for k in range(1, dp_size):
        dp_copy(k).wait_recv()

    @pl.loop(0, chips)
    def _(at):
        total = dp_sent[my_dp, at].astype(jnp.float32)
        for k in range(1, dp_size):
            total = total + dp_got[k - 1, at].astype(jnp.float32)
        held[at] = total

    def chip_copy(level):
        return remote(
            chip_sent.at[pl.ds(chips - 2 * (chips >> (level + 1)), chips >> (level + 1))],
            chip_got.at[pl.ds(chips - 2 * (chips >> (level + 1)), chips >> (level + 1))],
            chip_send.at[level],
            chip_recv.at[level],
            {"seq": (chip ^ (1 << level)) * 2 + core},
        )

    for level in range(chips.bit_length() - 1):
        left = chips >> (level + 1)
        base = chips - 2 * left
        bit = lax.rem(chip // (1 << level), 2)
        for at in range(left):
            chip_sent[base + at] = held[2 * at + 1 - bit].astype(jnp.bfloat16)
        chip_copy(level).start()
        chip_copy(level).wait_recv()
        for at in range(left):
            held[at] = held[2 * at + bit] + chip_got[base + at].astype(jnp.float32)
    final_ref[...] = held[0]

    pair_copy().wait_send()
    for k in range(1, dp_size):
        dp_copy(k).wait_send()
    for level in range(chips.bit_length() - 1):
        chip_copy(level).wait_send()

    @pl.loop(0, steps)
    def _(g):
        for source, target, send, recv in moved:
            for k in range(1, seq_size):
                spread(source, target, send, recv, g, k).wait_send()
        for k in range(1, seq_size):
            back(g, k).wait()
        back_own(g).wait()


def exchange_part(tokens, d_out, frames, frame_order, w_qkv, w_out, slots, seq_size, dp_size):
    row_count, width = tokens.shape
    slot_count = frame_order.shape[1]
    stripe = row_count // slot_count
    steps = stripe // GROUP
    rows = slot_count * GROUP
    chips = seq_size // 2
    levels = chips.bit_length() - 1
    tokens = tokens.reshape(slots, row_count // slots, width)
    d_out = d_out.reshape(tokens.shape)
    any_space = pl.BlockSpec(memory_space=pl.ANY)
    vmem = pl.BlockSpec(memory_space=pltpu.VMEM)
    smem = pl.BlockSpec(memory_space=pltpu.SMEM)
    narrow = jnp.bfloat16
    parts = (chips, width // seq_size, width // dp_size)
    crossing = pltpu.SemaphoreType.DMA((steps, seq_size))
    d_tokens, final = pl.pallas_call(
        functools.partial(exchange_kernel, 1.0 / math.sqrt(width // H), seq_size, dp_size),
        in_specs=[any_space, any_space, smem, vmem, any_space, any_space],
        out_specs=[any_space, vmem],
        out_shape=[
            jax.ShapeDtypeStruct(tokens.shape, narrow),
            jax.ShapeDtypeStruct(parts[1:], jnp.float32),
        ],
        scratch_shapes=[
            pltpu.VMEM(w_qkv.shape, narrow),
            pltpu.VMEM(w_out.shape, narrow),
            pltpu.VMEM((steps, slot_count, GROUP, width), narrow),
            pltpu.VMEM((steps, slot_count, GROUP, width), narrow),
            pltpu.VMEM((steps, slot_count, GROUP, width), narrow),
            pltpu.VMEM((rows, 3 * width), narrow),
            pltpu.VMEM((rows, width), narrow),
            pltpu.VMEM((rows, width), narrow),
            pltpu.VMEM((rows, 3 * width), narrow),
            pltpu.VMEM((width, width), jnp.float32),
            pltpu.VMEM((H, rows, rows), jnp.float32),
            pltpu.VMEM((rows, 1), jnp.float32),
            pltpu.VMEM((rows, rows), jnp.float32),
            pltpu.VMEM((dp_size, *parts), narrow),
            pltpu.VMEM((dp_size, *parts), narrow),
            pltpu.VMEM((dp_size, *parts), narrow),
            pltpu.VMEM((dp_size - 1, *parts), narrow),
            pltpu.VMEM(parts, jnp.float32),
            pltpu.VMEM((chips - 1, *parts[1:]), narrow),
            pltpu.VMEM((chips - 1, *parts[1:]), narrow),
            pltpu.SemaphoreType.DMA((2,)),
            crossing,
            crossing,
            crossing,
            crossing,
            crossing,
            crossing,
            pltpu.SemaphoreType.DMA((2,)),
            pltpu.SemaphoreType.DMA((dp_size - 1,)),
            pltpu.SemaphoreType.DMA((dp_size - 1,)),
            pltpu.SemaphoreType.DMA((levels,)),
            pltpu.SemaphoreType.DMA((levels,)),
        ],
        compiler_params=pltpu.CompilerParams(
            collective_id=0, has_side_effects=True, vmem_limit_bytes=60 * 2**20
        ),
    )(tokens, d_out, frames, frame_order, w_qkv, w_out)
    return d_tokens, final


def body(tokens, d_out, frames, frame_order, w_qkv, w_out):
    _, row_count, width = tokens.shape
    seq_size = lax.axis_size("seq")
    slot_count = frame_order.shape[1]
    stripe = row_count // slot_count
    patch_count = row_count * seq_size // slot_count
    slots = max(1, row_count // patch_count)
    piece = row_count // slots // seq_size
    live_slots = (frame_order[0] < frames[0]).astype(jnp.float32)

    dp_size = lax.axis_size("dp")
    if (
        piece == stripe
        and stripe % GROUP == 0
        and seq_size & (seq_size - 1) == 0
        and seq_size > 2
        and dp_size > 1
        and width % (16 * seq_size) == 0
    ):
        d_rows, final_out = exchange_part(
            tokens[0], d_out[0], frames, frame_order, w_qkv, w_out, slots, seq_size, dp_size
        )
        return (d_rows.reshape(tokens.shape), final_out)

    def spread(rows):
        sent = rows.reshape(slots, seq_size, piece, width)
        got = lax.all_to_all(sent, "seq", split_axis=1, concat_axis=0, tiled=True)
        return got.reshape(slot_count, stripe, width)

    d_rows, grad_out = local_part(spread(tokens), spread(d_out), live_slots, w_qkv, w_out)
    back = d_rows.reshape(seq_size * slots, 1, piece, width)
    d_tokens = lax.all_to_all(back, "seq", split_axis=0, concat_axis=1, tiled=True)
    share = lax.psum_scatter(
        grad_out.astype(jnp.bfloat16), "dp", scatter_dimension=1, tiled=True
    ).astype(jnp.float32)
    final_out = lax.psum_scatter(share, "seq", scatter_dimension=0, tiled=True)
    return (d_tokens.reshape(tokens.shape), final_out)


def solution(mesh):
    placed = (P("dp", "seq", None), P("dp", "seq", None), P("dp"), P("dp", None), P(), P())
    return jax.shard_map(
        body,
        mesh=mesh,
        in_specs=placed,
        out_specs=(P("dp", "seq", None), P("seq", "dp")),
        check_vma=False,
    )
```

```python
import functools
import math

import jax
import jax.numpy as jnp
from jax import lax
from jax.experimental import pallas as pl
from jax.experimental.pallas import tpu as pltpu
from jax.sharding import PartitionSpec as P

H = 16
LANES = 128
GROUP = 8
AHEAD = 3
VMEM_BYTES = 50 * 2**20
SUBLANES = 16
NT = (((1,), (1,)), ((), ()))
TN = (((0,), (0,)), ((), ()))


def dot(a, b, dims=(((1,), (0,)), ((), ()))):
    return lax.dot_general(a, b, dims, preferred_element_type=jnp.float32)


def attend(joined, head_grad, mask, attended, qkv_grad, width, score_scale):
    head_dim = width // H
    column = lax.broadcasted_iota(jnp.int32, (1, 2 * LANES), 1)
    pending = [{}, {}, {}, {}]
    for h in range(H):
        low, high = h * head_dim, (h + 1) * head_dim
        first, last = low // LANES, -(-high // LANES)
        start, size = first * LANES, (last - first) * LANES
        keep = jnp.where(
            (column[:, :size] >= low - start) & (column[:, :size] < high - start), 1.0, 0.0
        ).astype(jnp.bfloat16)
        q = joined[:, start : start + size] * keep
        k = joined[:, width + start : width + start + size] * keep
        v = joined[:, 2 * width + start : 2 * width + start + size] * keep
        g = head_grad[:, start : start + size] * keep
        scores = dot(q, k, NT) * score_scale + mask
        exponent = jnp.exp(scores - jnp.max(scores, axis=-1, keepdims=True))
        probs = exponent * (1.0 / jnp.sum(exponent, axis=-1, keepdims=True))
        rounded = probs.astype(jnp.bfloat16)
        prob_grad = dot(g, v, NT)
        inner = jnp.sum(probs * prob_grad, axis=-1, keepdims=True)
        score_grad = (probs * (prob_grad - inner) * score_scale).astype(jnp.bfloat16)
        results = (
            dot(rounded, v),
            dot(score_grad, k),
            dot(score_grad, q, TN),
            dot(rounded, g, TN),
        )
        for which, result in enumerate(results):
            for tile in range(first, last):
                piece = result[:, (tile - first) * LANES : (tile - first + 1) * LANES]
                held = pending[which].pop(tile, None)
                piece = piece if held is None else held + piece
                if (tile + 1) * LANES <= high:
                    piece = piece.astype(jnp.bfloat16)
                    if which == 0:
                        attended[:, tile * LANES : (tile + 1) * LANES] = piece
                    else:
                        at = (which - 1) * width + tile * LANES
                        qkv_grad[:, at : at + LANES] = piece
                else:
                    pending[which][tile] = piece


def kernel(
    score_scale,
    tokens_ref,
    d_out_ref,
    live_ref,
    mask_ref,
    w_qkv_ref,
    w_out_ref,
    d_tokens_ref,
    grad_ref,
    joined,
    head_grad,
    attended,
    qkv_grad,
):
    rows, width = attended.shape
    values = tokens_ref[...].astype(jnp.float32).reshape(rows, width)
    center = values - jnp.mean(values, axis=-1, keepdims=True)
    inverse = lax.rsqrt(jnp.mean(center * center, axis=-1, keepdims=True) + 1e-06)
    normalized = center * inverse
    normed = normalized.astype(jnp.bfloat16)
    masked_wide = d_out_ref[...].astype(jnp.float32).reshape(rows, width) * live_ref[...]
    masked = masked_wide.astype(jnp.bfloat16)
    joined[...] = dot(normed, w_qkv_ref[...]).astype(jnp.bfloat16)
    head_grad[...] = dot(masked, w_out_ref[...], NT).astype(jnp.bfloat16)
    attend(joined, head_grad, mask_ref[...], attended, qkv_grad, width, score_scale)
    term = dot(attended[...], masked, TN)

    @pl.when(pl.program_id(0) == 0)
    def _():
        grad_ref[...] = term

    @pl.when(pl.program_id(0) != 0)
    def _():
        grad_ref[...] += term

    normed_grad = dot(qkv_grad[...], w_qkv_ref[...], NT)
    mean_grad = jnp.mean(normed_grad, axis=-1, keepdims=True)
    mean_cross = jnp.mean(normed_grad * normalized, axis=-1, keepdims=True)
    result = masked_wide + inverse * (normed_grad - mean_grad - normalized * mean_cross)
    d_tokens_ref[...] = result.reshape(d_tokens_ref.shape).astype(jnp.bfloat16)


def mask_of(live_slots, rows, group):
    at = jnp.arange(rows, dtype=jnp.int32)
    live_rows = jnp.repeat(live_slots, group)
    mask = jnp.where(
        (at[:, None] % group == at[None, :] % group) & (live_rows[None, :] > 0.5), 0.0, -1e30
    ).astype(jnp.float32)
    return live_rows, mask


def local_part(tokens, d_out, live_slots, w_qkv, w_out):
    slot_count, stripe, width = tokens.shape
    group = min(GROUP, stripe)
    rows = slot_count * group
    steps = stripe // group
    live_rows, mask = mask_of(live_slots, rows, group)
    if steps == 1:
        tokens, d_out = tokens.reshape(rows, width), d_out.reshape(rows, width)
        moving = pl.BlockSpec((rows, width), lambda i: (0, 0))
    else:
        moving = pl.BlockSpec((slot_count, group, width), lambda i: (0, i, 0))

    def whole(shape):
        return pl.BlockSpec(shape, lambda i: (0, 0), pipeline_mode=pl.Buffered(1))

    d_tokens, grad = pl.pallas_call(
        functools.partial(kernel, 1.0 / math.sqrt(width // H)),
        grid=(steps,),
        in_specs=[
            moving,
            moving,
            whole((rows, 1)),
            whole((rows, rows)),
            whole(w_qkv.shape),
            whole(w_out.shape),
        ],
        out_specs=[moving, whole((width, width))],
        out_shape=[
            jax.ShapeDtypeStruct(tokens.shape, jnp.bfloat16),
            jax.ShapeDtypeStruct((width, width), jnp.float32),
        ],
        scratch_shapes=[
            pltpu.VMEM((rows, 3 * width), jnp.bfloat16),
            pltpu.VMEM((rows, width), jnp.bfloat16),
            pltpu.VMEM((rows, width), jnp.bfloat16),
            pltpu.VMEM((rows, 3 * width), jnp.bfloat16),
        ],
        compiler_params=pltpu.CompilerParams(
            dimension_semantics=("arbitrary",), vmem_limit_bytes=60 * 2**20
        ),
    )(tokens, d_out, live_rows[:, None], mask, w_qkv, w_out)
    return d_tokens.reshape(slot_count, stripe, width), grad


def mask_in_kernel(group, order, count):
    rows = order.shape[1] * group
    live = (order < count).astype(jnp.float32)
    slot_of = lax.broadcasted_iota(jnp.int32, (rows, order.shape[1]), 1) * group
    row_of = lax.broadcasted_iota(jnp.int32, slot_of.shape, 0)
    owns = (row_of >= slot_of) & (row_of < slot_of + group)
    live_rows = jnp.sum(jnp.where(owns, live, 0.0), axis=-1, keepdims=True)
    live_columns = dot(jnp.broadcast_to(live, (8, order.shape[1])), owns.astype(jnp.float32), NT)
    row = lax.broadcasted_iota(jnp.int32, (rows, rows), 0)
    column = lax.broadcasted_iota(jnp.int32, (rows, rows), 1)
    same = lax.rem(row, group) == lax.rem(column, group)
    mask = jnp.where(same & (live_columns[:1] > 0.5), 0.0, -1e30)
    return live_rows, mask


def head_window(width, h):
    head_dim = width // H
    low, high = h * head_dim, (h + 1) * head_dim
    first, last = low // LANES, -(-high // LANES)
    start, size = first * LANES, (last - first) * LANES
    column = lax.broadcasted_iota(jnp.int32, (1, 2 * LANES), 1)
    keep = jnp.where(
        (column[:, :size] >= low - start) & (column[:, :size] < high - start), 1.0, 0.0
    ).astype(jnp.bfloat16)
    return start, size, high, keep


def put_head(pending, result, start, size, high, target, offset):
    for tile in range(start // LANES, (start + size) // LANES):
        piece = result[:, tile * LANES - start : (tile + 1) * LANES - start]
        held = pending.pop(tile, None)
        piece = piece if held is None else held + piece
        if (tile + 1) * LANES <= high:
            at = offset + tile * LANES
            target[:, at : at + LANES] = piece.astype(jnp.bfloat16)
        else:
            pending[tile] = piece


def attend_forward(joined, mask, attended, probs_ref, width, score_scale):
    pending = {}
    for h in range(H):
        start, size, high, keep = head_window(width, h)
        q = joined[:, start : start + size] * keep
        k = joined[:, width + start : width + start + size]
        v = joined[:, 2 * width + start : 2 * width + start + size] * keep
        scores = dot(q, k, NT) * score_scale + mask
        exponent = jnp.exp(scores - jnp.max(scores, axis=-1, keepdims=True))
        probs = exponent * (1.0 / jnp.sum(exponent, axis=-1, keepdims=True))
        probs_ref[h] = probs
        result = dot(probs.astype(jnp.bfloat16), v)
        put_head(pending, result, start, size, high, attended, 0)


def attend_backward(joined, head_grad, probs_ref, qkv_grad, width, score_scale):
    pending = [{}, {}, {}]
    for h in range(H):
        start, size, high, keep = head_window(width, h)
        q = joined[:, start : start + size] * keep
        k = joined[:, width + start : width + start + size] * keep
        v = joined[:, 2 * width + start : 2 * width + start + size]
        g = head_grad[:, start : start + size] * keep
        probs = probs_ref[h]
        prob_grad = dot(g, v, NT)
        inner = jnp.sum(probs * prob_grad, axis=-1, keepdims=True)
        score_grad = (probs * (prob_grad - inner) * score_scale).astype(jnp.bfloat16)
        results = (
            dot(score_grad, k),
            dot(score_grad, q, TN),
            dot(probs.astype(jnp.bfloat16), g, TN),
        )
        for which, result in enumerate(results):
            put_head(pending[which], result, start, size, high, qkv_grad, which * width)


def fold_of(row_block, column_block):
    rest = column_block % LANES
    fits = [f for f in range(1, LANES // max(rest, 1) + 1) if row_block % (f * SUBLANES) == 0]
    return column_block // LANES, rest, fits[-1] if fits else 1


def folded_rows(row_block, column_block):
    full, rest, fold = fold_of(row_block, column_block)
    return full * row_block + (row_block // fold if rest else 0)


def fold_piece(value):
    full, rest, fold = fold_of(*value.shape)
    tiles = [value[:, t * LANES : (t + 1) * LANES] for t in range(full)]
    if rest:
        size = value.shape[0] // fold
        parts = [value[f * size : (f + 1) * size, full * LANES :] for f in range(fold)]
        if rest * fold < LANES:
            parts.append(jnp.zeros((size, LANES - rest * fold), value.dtype))
        tiles.append(jnp.concatenate(parts, axis=1))
    return tiles


def unfold_piece(value, target):
    row_block, column_block = target.shape
    full, rest, fold = fold_of(row_block, column_block)
    for t in range(full):
        target[:, t * LANES : (t + 1) * LANES] = value[t * row_block : (t + 1) * row_block]
    if rest:
        size = row_block // fold
        tail = value[full * row_block :]
        for f in range(fold):
            target[f * size : (f + 1) * size, full * LANES :] = tail[:, f * rest : (f + 1) * rest]


def exchange_kernel(
    score_scale,
    seq_size,
    dp_size,
    tokens_ref,
    d_out_ref,
    count_ref,
    order_ref,
    w_qkv_hbm,
    w_out_hbm,
    d_tokens_ref,
    final_ref,
    w_qkv_ref,
    w_out_ref,
    got_tokens,
    got_d_out,
    results,
    joined,
    head_grad,
    attended,
    qkv_grad,
    grad,
    probs_ref,
    live_ref,
    mask_ref,
    pair_sent,
    pair_got,
    dp_sent,
    dp_got,
    held,
    chip_sent,
    chip_got,
    weight_sems,
    tokens_send,
    tokens_recv,
    d_out_send,
    d_out_recv,
    back_send,
    back_recv,
    pair_sems,
    dp_send,
    dp_recv,
    chip_send,
    chip_recv,
):
    rows, width = attended.shape
    steps, slot_count, group, _ = got_tokens.shape
    slots = tokens_ref.shape[0]
    stripe = steps * group
    chips = seq_size // 2
    row_block, column_block = final_ref.shape
    me = lax.axis_index("seq")
    my_dp = lax.axis_index("dp")
    core = lax.rem(me, 2)
    chip = me // 2
    far_first = tuple(reversed(range(1, seq_size)))

    def peer(k):
        return me ^ k

    def dp_peer(k):
        return lax.rem(my_dp + k, dp_size)

    barrier = pltpu.get_barrier_semaphore()
    for k in range(1, seq_size):
        pl.semaphore_signal(
            barrier,
            inc=1,
            device_id={"seq": peer(k)},
            device_id_type=pl.DeviceIdType.MESH,
        )
    for k in range(1, dp_size):
        pl.semaphore_signal(
            barrier,
            inc=1,
            device_id={"dp": dp_peer(k)},
            device_id_type=pl.DeviceIdType.MESH,
        )
    pl.semaphore_wait(barrier, seq_size - 1 + dp_size - 1)

    def remote(source, target, send, recv, device):
        return pltpu.make_async_remote_copy(
            src_ref=source,
            dst_ref=target,
            send_sem=send,
            recv_sem=recv,
            device_id=device,
            device_id_type=pl.DeviceIdType.MESH,
        )

    def home(ref, owner, g):
        return ref.at[:, pl.ds(pl.multiple_of(owner * stripe + g * group, group), group), :]

    def away(ref, owner, g):
        return ref.at[g, pl.ds(owner * slots, slots)]

    def spread(source, target, send, recv, g, k):
        return remote(
            home(source, peer(k), g),
            away(target, me, g),
            send.at[g, k],
            recv.at[g, k],
            {"seq": peer(k)},
        )

    def keep_own(source, target, recv, g):
        return pltpu.make_async_copy(home(source, me, g), away(target, me, g), recv.at[g, 0])

    def back(g, k):
        return remote(
            away(results, peer(k), g),
            home(d_tokens_ref, me, g),
            back_send.at[g, k],
            back_recv.at[g, k],
            {"seq": peer(k)},
        )

    def back_own(g):
        return pltpu.make_async_copy(
            away(results, me, g), home(d_tokens_ref, me, g), back_recv.at[g, 0]
        )

    moved = (
        (tokens_ref, got_tokens, tokens_send, tokens_recv),
        (d_out_ref, got_d_out, d_out_send, d_out_recv),
    )

    def depart(which, g):
        source, target, send, recv = moved[which]
        for k in far_first:
            spread(source, target, send, recv, g, k).start()
        keep_own(source, target, recv, g).start()

    def arrived(which, g):
        source, target, send, recv = moved[which]
        for k in far_first:
            spread(source, target, send, recv, g, k).wait_recv()
        keep_own(source, target, recv, g).wait()

    def give_back(g):
        for k in far_first:
            back(g, k).start()
        back_own(g).start()

    for at in range(min(AHEAD, 2 * steps)):
        depart(at % 2, at // 2)
    weights = (
        pltpu.make_async_copy(w_qkv_hbm, w_qkv_ref, weight_sems.at[0]),
        pltpu.make_async_copy(w_out_hbm, w_out_ref, weight_sems.at[1]),
    )
    for copy in weights:
        copy.start()
    live_ref[...], mask_ref[...] = mask_in_kernel(group, order_ref[...], count_ref[0])
    grad[...] = jnp.zeros_like(grad)
    for copy in weights:
        copy.wait()

    def depart_next(which, g):
        at = AHEAD + which
        later = g + at // 2

        @pl.when(later < steps)
        def _():
            depart(at % 2, later)

    def pair_copy():
        return remote(
            pair_sent, pair_got, pair_sems.at[0], pair_sems.at[1], {"seq": chip * 2 + 1 - core}
        )

    def row_piece(at, parity):
        start = pl.multiple_of((at * 2 + parity) * row_block, row_block)
        return grad[pl.ds(start, row_block), :]

    def pieces_of(value, d):
        start = 0
        for tile in fold_piece(value[:, d * column_block : (d + 1) * column_block]):
            yield slice(start, start + tile.shape[0]), tile
            start += tile.shape[0]

    def dp_copy(k):
        return remote(
            dp_sent.at[dp_peer(k)],
            dp_got.at[k - 1],
            dp_send.at[k - 1],
            dp_recv.at[k - 1],
            {"dp": dp_peer(k)},
        )

    @pl.loop(0, steps)
    def _(g):
        arrived(0, g)
        depart_next(0, g)
        values = got_tokens[g].astype(jnp.float32).reshape(rows, width)
        center = values - jnp.mean(values, axis=-1, keepdims=True)
        inverse = lax.rsqrt(jnp.mean(center * center, axis=-1, keepdims=True) + 1e-06)
        normalized = center * inverse
        joined[...] = dot(normalized.astype(jnp.bfloat16), w_qkv_ref[...]).astype(jnp.bfloat16)
        attend_forward(joined, mask_ref[...], attended, probs_ref, width, score_scale)

        @pl.when(g == steps - 1)
        def _():
            for earlier in range(max(steps - 3, 0)):
                give_back(earlier)

        arrived(1, g)
        depart_next(1, g)
        masked_wide = got_d_out[g].astype(jnp.float32).reshape(rows, width) * live_ref[...]
        masked = masked_wide.astype(jnp.bfloat16)
        grad[...] += dot(attended[...], masked, TN)

        @pl.when(g == steps - 1)
        def _():
            @pl.loop(0, chips)
            def _(at):
                value = row_piece(at, 1 - core)
                for d in range(dp_size):
                    for where, tile in pieces_of(value, d):
                        pair_sent[d, at, where] = tile.astype(jnp.bfloat16)

            pair_copy().start()

        head_grad[...] = dot(masked, w_out_ref[...], NT).astype(jnp.bfloat16)

        @pl.when(g == steps - 1)
        def _():
            pair_copy().wait_recv()

            @pl.loop(0, chips)
            def _(at):
                value = row_piece(at, core)
                for d in range(dp_size):
                    for where, tile in pieces_of(value, d):
                        total = tile + pair_got[d, at, where].astype(jnp.float32)
                        dp_sent[d, at, where] = total.astype(jnp.bfloat16)

            for k in range(1, dp_size):
                dp_copy(k).start()

            for earlier in range(max(steps - 3, 0), steps - 1):
                give_back(earlier)

        attend_backward(joined, head_grad, probs_ref, qkv_grad, width, score_scale)
        normed_grad = dot(qkv_grad[...], w_qkv_ref[...], NT)
        mean_grad = jnp.mean(normed_grad, axis=-1, keepdims=True)
        mean_cross = jnp.mean(normed_grad * normalized, axis=-1, keepdims=True)
        result = masked_wide + inverse * (normed_grad - mean_grad - normalized * mean_cross)
        results[g] = result.reshape(slot_count, group, width).astype(jnp.bfloat16)

    give_back(steps - 1)
    for k in range(1, dp_size):
        dp_copy(k).wait_recv()

    @pl.loop(0, chips)
    def _(at):
        total = dp_sent[my_dp, at].astype(jnp.float32)
        for k in range(1, dp_size):
            total = total + dp_got[k - 1, at].astype(jnp.float32)
        held[at] = total

    def chip_copy(level):
        return remote(
            chip_sent.at[pl.ds(chips - 2 * (chips >> (level + 1)), chips >> (level + 1))],
            chip_got.at[pl.ds(chips - 2 * (chips >> (level + 1)), chips >> (level + 1))],
            chip_send.at[level],
            chip_recv.at[level],
            {"seq": (chip ^ (1 << level)) * 2 + core},
        )

    for level in range(chips.bit_length() - 1):
        left = chips >> (level + 1)
        base = chips - 2 * left
        bit = lax.rem(chip // (1 << level), 2)
        for at in range(left):
            chip_sent[base + at] = held[2 * at + 1 - bit].astype(jnp.bfloat16)
        chip_copy(level).start()
        chip_copy(level).wait_recv()
        for at in range(left):
            held[at] = held[2 * at + bit] + chip_got[base + at].astype(jnp.float32)
    unfold_piece(held[0], final_ref)

    pair_copy().wait_send()
    for k in range(1, dp_size):
        dp_copy(k).wait_send()
    for level in range(chips.bit_length() - 1):
        chip_copy(level).wait_send()

    @pl.loop(0, steps)
    def _(g):
        for source, target, send, recv in moved:
            for k in range(1, seq_size):
                spread(source, target, send, recv, g, k).wait_send()
        for k in range(1, seq_size):
            back(g, k).wait()
        back_own(g).wait()


def exchange_part(tokens, d_out, frames, frame_order, w_qkv, w_out, slots, seq_size, dp_size):
    row_count, width = tokens.shape
    slot_count = frame_order.shape[1]
    stripe = row_count // slot_count
    steps = stripe // GROUP
    rows = slot_count * GROUP
    chips = seq_size // 2
    levels = chips.bit_length() - 1
    tokens = tokens.reshape(slots, row_count // slots, width)
    d_out = d_out.reshape(tokens.shape)
    any_space = pl.BlockSpec(memory_space=pl.ANY)
    vmem = pl.BlockSpec(memory_space=pltpu.VMEM)
    smem = pl.BlockSpec(memory_space=pltpu.SMEM)
    narrow = jnp.bfloat16
    share = (width // seq_size, width // dp_size)
    parts = (chips, folded_rows(*share), LANES)
    crossing = pltpu.SemaphoreType.DMA((steps, seq_size))
    d_tokens, final = pl.pallas_call(
        functools.partial(exchange_kernel, 1.0 / math.sqrt(width // H), seq_size, dp_size),
        in_specs=[any_space, any_space, smem, vmem, any_space, any_space],
        out_specs=[any_space, vmem],
        out_shape=[
            jax.ShapeDtypeStruct(tokens.shape, narrow),
            jax.ShapeDtypeStruct(share, jnp.float32),
        ],
        scratch_shapes=[
            pltpu.VMEM(w_qkv.shape, narrow),
            pltpu.VMEM(w_out.shape, narrow),
            pltpu.VMEM((steps, slot_count, GROUP, width), narrow),
            pltpu.VMEM((steps, slot_count, GROUP, width), narrow),
            pltpu.VMEM((steps, slot_count, GROUP, width), narrow),
            pltpu.VMEM((rows, 3 * width), narrow),
            pltpu.VMEM((rows, width), narrow),
            pltpu.VMEM((rows, width), narrow),
            pltpu.VMEM((rows, 3 * width), narrow),
            pltpu.VMEM((width, width), jnp.float32),
            pltpu.VMEM((H, rows, rows), jnp.float32),
            pltpu.VMEM((rows, 1), jnp.float32),
            pltpu.VMEM((rows, rows), jnp.float32),
            pltpu.VMEM((dp_size, *parts), narrow),
            pltpu.VMEM((dp_size, *parts), narrow),
            pltpu.VMEM((dp_size, *parts), narrow),
            pltpu.VMEM((dp_size - 1, *parts), narrow),
            pltpu.VMEM(parts, jnp.float32),
            pltpu.VMEM((chips - 1, *parts[1:]), narrow),
            pltpu.VMEM((chips - 1, *parts[1:]), narrow),
            pltpu.SemaphoreType.DMA((2,)),
            crossing,
            crossing,
            crossing,
            crossing,
            crossing,
            crossing,
            pltpu.SemaphoreType.DMA((2,)),
            pltpu.SemaphoreType.DMA((dp_size - 1,)),
            pltpu.SemaphoreType.DMA((dp_size - 1,)),
            pltpu.SemaphoreType.DMA((levels,)),
            pltpu.SemaphoreType.DMA((levels,)),
        ],
        compiler_params=pltpu.CompilerParams(
            collective_id=0, has_side_effects=True, vmem_limit_bytes=VMEM_BYTES
        ),
    )(tokens, d_out, frames, frame_order, w_qkv, w_out)
    return d_tokens, final


def body(tokens, d_out, frames, frame_order, w_qkv, w_out):
    _, row_count, width = tokens.shape
    seq_size = lax.axis_size("seq")
    slot_count = frame_order.shape[1]
    stripe = row_count // slot_count
    patch_count = row_count * seq_size // slot_count
    slots = max(1, row_count // patch_count)
    piece = row_count // slots // seq_size
    live_slots = (frame_order[0] < frames[0]).astype(jnp.float32)

    dp_size = lax.axis_size("dp")
    if (
        piece == stripe
        and stripe % GROUP == 0
        and seq_size & (seq_size - 1) == 0
        and seq_size > 2
        and dp_size > 1
        and width % (16 * seq_size) == 0
    ):
        d_rows, final_out = exchange_part(
            tokens[0], d_out[0], frames, frame_order, w_qkv, w_out, slots, seq_size, dp_size
        )
        return (d_rows.reshape(tokens.shape), final_out)

    def spread(rows):
        sent = rows.reshape(slots, seq_size, piece, width)
        got = lax.all_to_all(sent, "seq", split_axis=1, concat_axis=0, tiled=True)
        return got.reshape(slot_count, stripe, width)

    d_rows, grad_out = local_part(spread(tokens), spread(d_out), live_slots, w_qkv, w_out)
    back = d_rows.reshape(seq_size * slots, 1, piece, width)
    d_tokens = lax.all_to_all(back, "seq", split_axis=0, concat_axis=1, tiled=True)
    share = lax.psum_scatter(
        grad_out.astype(jnp.bfloat16), "dp", scatter_dimension=1, tiled=True
    ).astype(jnp.float32)
    final_out = lax.psum_scatter(share, "seq", scatter_dimension=0, tiled=True)
    return (d_tokens.reshape(tokens.shape), final_out)


def solution(mesh):
    placed = (P("dp", "seq", None), P("dp", "seq", None), P("dp"), P("dp", None), P(), P())
    return jax.shard_map(
        body,
        mesh=mesh,
        in_specs=placed,
        out_specs=(P("dp", "seq", None), P("seq", "dp")),
        check_vma=False,
    )
```

```python
import functools
import math

import jax
import jax.numpy as jnp
from jax import lax
from jax.experimental import pallas as pl
from jax.experimental.pallas import tpu as pltpu
from jax.sharding import PartitionSpec as P

H = 16
LANES = 128
GROUP = 8
AHEAD = 3
VMEM_BYTES = 50 * 2**20
SUBLANES = 16
NT = (((1,), (1,)), ((), ()))
TN = (((0,), (0,)), ((), ()))


def dot(a, b, dims=(((1,), (0,)), ((), ()))):
    return lax.dot_general(a, b, dims, preferred_element_type=jnp.float32)


def attend(joined, head_grad, mask, attended, qkv_grad, width, score_scale):
    head_dim = width // H
    column = lax.broadcasted_iota(jnp.int32, (1, 2 * LANES), 1)
    pending = [{}, {}, {}, {}]
    for h in range(H):
        low, high = h * head_dim, (h + 1) * head_dim
        first, last = low // LANES, -(-high // LANES)
        start, size = first * LANES, (last - first) * LANES
        keep = jnp.where(
            (column[:, :size] >= low - start) & (column[:, :size] < high - start), 1.0, 0.0
        ).astype(jnp.bfloat16)
        q = joined[:, start : start + size] * keep
        k = joined[:, width + start : width + start + size] * keep
        v = joined[:, 2 * width + start : 2 * width + start + size] * keep
        g = head_grad[:, start : start + size] * keep
        scores = dot(q, k, NT) * score_scale + mask
        exponent = jnp.exp(scores - jnp.max(scores, axis=-1, keepdims=True))
        probs = exponent * (1.0 / jnp.sum(exponent, axis=-1, keepdims=True))
        rounded = probs.astype(jnp.bfloat16)
        prob_grad = dot(g, v, NT)
        inner = jnp.sum(probs * prob_grad, axis=-1, keepdims=True)
        score_grad = (probs * (prob_grad - inner) * score_scale).astype(jnp.bfloat16)
        results = (
            dot(rounded, v),
            dot(score_grad, k),
            dot(score_grad, q, TN),
            dot(rounded, g, TN),
        )
        for which, result in enumerate(results):
            for tile in range(first, last):
                piece = result[:, (tile - first) * LANES : (tile - first + 1) * LANES]
                held = pending[which].pop(tile, None)
                piece = piece if held is None else held + piece
                if (tile + 1) * LANES <= high:
                    piece = piece.astype(jnp.bfloat16)
                    if which == 0:
                        attended[:, tile * LANES : (tile + 1) * LANES] = piece
                    else:
                        at = (which - 1) * width + tile * LANES
                        qkv_grad[:, at : at + LANES] = piece
                else:
                    pending[which][tile] = piece


def kernel(
    score_scale,
    tokens_ref,
    d_out_ref,
    live_ref,
    mask_ref,
    w_qkv_ref,
    w_out_ref,
    d_tokens_ref,
    grad_ref,
    joined,
    head_grad,
    attended,
    qkv_grad,
):
    rows, width = attended.shape
    values = tokens_ref[...].astype(jnp.float32).reshape(rows, width)
    center = values - jnp.mean(values, axis=-1, keepdims=True)
    inverse = lax.rsqrt(jnp.mean(center * center, axis=-1, keepdims=True) + 1e-06)
    normalized = center * inverse
    normed = normalized.astype(jnp.bfloat16)
    masked_wide = d_out_ref[...].astype(jnp.float32).reshape(rows, width) * live_ref[...]
    masked = masked_wide.astype(jnp.bfloat16)
    joined[...] = dot(normed, w_qkv_ref[...]).astype(jnp.bfloat16)
    head_grad[...] = dot(masked, w_out_ref[...], NT).astype(jnp.bfloat16)
    attend(joined, head_grad, mask_ref[...], attended, qkv_grad, width, score_scale)
    term = dot(attended[...], masked, TN)

    @pl.when(pl.program_id(0) == 0)
    def _():
        grad_ref[...] = term

    @pl.when(pl.program_id(0) != 0)
    def _():
        grad_ref[...] += term

    normed_grad = dot(qkv_grad[...], w_qkv_ref[...], NT)
    mean_grad = jnp.mean(normed_grad, axis=-1, keepdims=True)
    mean_cross = jnp.mean(normed_grad * normalized, axis=-1, keepdims=True)
    result = masked_wide + inverse * (normed_grad - mean_grad - normalized * mean_cross)
    d_tokens_ref[...] = result.reshape(d_tokens_ref.shape).astype(jnp.bfloat16)


def mask_of(live_slots, rows, group):
    at = jnp.arange(rows, dtype=jnp.int32)
    live_rows = jnp.repeat(live_slots, group)
    mask = jnp.where(
        (at[:, None] % group == at[None, :] % group) & (live_rows[None, :] > 0.5), 0.0, -1e30
    ).astype(jnp.float32)
    return live_rows, mask


def local_part(tokens, d_out, live_slots, w_qkv, w_out):
    slot_count, stripe, width = tokens.shape
    group = min(GROUP, stripe)
    rows = slot_count * group
    steps = stripe // group
    live_rows, mask = mask_of(live_slots, rows, group)
    if steps == 1:
        tokens, d_out = tokens.reshape(rows, width), d_out.reshape(rows, width)
        moving = pl.BlockSpec((rows, width), lambda i: (0, 0))
    else:
        moving = pl.BlockSpec((slot_count, group, width), lambda i: (0, i, 0))

    def whole(shape):
        return pl.BlockSpec(shape, lambda i: (0, 0), pipeline_mode=pl.Buffered(1))

    d_tokens, grad = pl.pallas_call(
        functools.partial(kernel, 1.0 / math.sqrt(width // H)),
        grid=(steps,),
        in_specs=[
            moving,
            moving,
            whole((rows, 1)),
            whole((rows, rows)),
            whole(w_qkv.shape),
            whole(w_out.shape),
        ],
        out_specs=[moving, whole((width, width))],
        out_shape=[
            jax.ShapeDtypeStruct(tokens.shape, jnp.bfloat16),
            jax.ShapeDtypeStruct((width, width), jnp.float32),
        ],
        scratch_shapes=[
            pltpu.VMEM((rows, 3 * width), jnp.bfloat16),
            pltpu.VMEM((rows, width), jnp.bfloat16),
            pltpu.VMEM((rows, width), jnp.bfloat16),
            pltpu.VMEM((rows, 3 * width), jnp.bfloat16),
        ],
        compiler_params=pltpu.CompilerParams(
            dimension_semantics=("arbitrary",), vmem_limit_bytes=60 * 2**20
        ),
    )(tokens, d_out, live_rows[:, None], mask, w_qkv, w_out)
    return d_tokens.reshape(slot_count, stripe, width), grad


def mask_in_kernel(group, order, count):
    rows = order.shape[1] * group
    live = (order < count).astype(jnp.float32)
    slot_of = lax.broadcasted_iota(jnp.int32, (rows, order.shape[1]), 1) * group
    row_of = lax.broadcasted_iota(jnp.int32, slot_of.shape, 0)
    owns = (row_of >= slot_of) & (row_of < slot_of + group)
    live_rows = jnp.sum(jnp.where(owns, live, 0.0), axis=-1, keepdims=True)
    live_columns = dot(jnp.broadcast_to(live, (8, order.shape[1])), owns.astype(jnp.float32), NT)
    row = lax.broadcasted_iota(jnp.int32, (rows, rows), 0)
    column = lax.broadcasted_iota(jnp.int32, (rows, rows), 1)
    same = lax.rem(row, group) == lax.rem(column, group)
    mask = jnp.where(same & (live_columns[:1] > 0.5), 0.0, -1e30)
    return live_rows, mask


def head_window(width, h):
    head_dim = width // H
    low, high = h * head_dim, (h + 1) * head_dim
    first, last = low // LANES, -(-high // LANES)
    start, size = first * LANES, (last - first) * LANES
    column = lax.broadcasted_iota(jnp.int32, (1, 2 * LANES), 1)
    keep = jnp.where(
        (column[:, :size] >= low - start) & (column[:, :size] < high - start), 1.0, 0.0
    ).astype(jnp.bfloat16)
    return start, size, high, keep


def put_head(pending, result, start, size, high, target, offset):
    for tile in range(start // LANES, (start + size) // LANES):
        piece = result[:, tile * LANES - start : (tile + 1) * LANES - start]
        held = pending.pop(tile, None)
        piece = piece if held is None else held + piece
        if (tile + 1) * LANES <= high:
            at = offset + tile * LANES
            target[:, at : at + LANES] = piece.astype(jnp.bfloat16)
        else:
            pending[tile] = piece


def attend_forward(joined, mask, attended, probs_ref, width, score_scale):
    pending = {}
    for h in range(H):
        start, size, high, keep = head_window(width, h)
        q = joined[:, start : start + size] * keep
        k = joined[:, width + start : width + start + size]
        v = joined[:, 2 * width + start : 2 * width + start + size] * keep
        scores = dot(q, k, NT) * score_scale + mask
        exponent = jnp.exp(scores - jnp.max(scores, axis=-1, keepdims=True))
        probs = exponent * (1.0 / jnp.sum(exponent, axis=-1, keepdims=True))
        probs_ref[h] = probs
        result = dot(probs.astype(jnp.bfloat16), v)
        put_head(pending, result, start, size, high, attended, 0)


def attend_backward(joined, head_grad, probs_ref, qkv_grad, width, score_scale):
    pending = [{}, {}, {}]
    for h in range(H):
        start, size, high, keep = head_window(width, h)
        q = joined[:, start : start + size] * keep
        k = joined[:, width + start : width + start + size] * keep
        v = joined[:, 2 * width + start : 2 * width + start + size]
        g = head_grad[:, start : start + size] * keep
        probs = probs_ref[h]
        prob_grad = dot(g, v, NT)
        inner = jnp.sum(probs * prob_grad, axis=-1, keepdims=True)
        score_grad = (probs * (prob_grad - inner) * score_scale).astype(jnp.bfloat16)
        results = (
            dot(score_grad, k),
            dot(score_grad, q, TN),
            dot(probs.astype(jnp.bfloat16), g, TN),
        )
        for which, result in enumerate(results):
            put_head(pending[which], result, start, size, high, qkv_grad, which * width)


def fold_of(row_block, column_block):
    rest = column_block % LANES
    fits = [f for f in range(1, LANES // max(rest, 1) + 1) if row_block % (f * SUBLANES) == 0]
    return column_block // LANES, rest, fits[-1] if fits else 1


def folded_rows(row_block, column_block):
    full, rest, fold = fold_of(row_block, column_block)
    return full * row_block + (row_block // fold if rest else 0)


def fold_piece(value):
    full, rest, fold = fold_of(*value.shape)
    tiles = [value[:, t * LANES : (t + 1) * LANES] for t in range(full)]
    if rest:
        size = value.shape[0] // fold
        parts = [value[f * size : (f + 1) * size, full * LANES :] for f in range(fold)]
        if rest * fold < LANES:
            parts.append(jnp.zeros((size, LANES - rest * fold), value.dtype))
        tiles.append(jnp.concatenate(parts, axis=1))
    return tiles


def unfold_piece(value, target):
    row_block, column_block = target.shape
    full, rest, fold = fold_of(row_block, column_block)
    for t in range(full):
        target[:, t * LANES : (t + 1) * LANES] = value[t * row_block : (t + 1) * row_block]
    if rest:
        size = row_block // fold
        tail = value[full * row_block :]
        for f in range(fold):
            target[f * size : (f + 1) * size, full * LANES :] = tail[:, f * rest : (f + 1) * rest]


def exchange_kernel(
    score_scale,
    seq_size,
    dp_size,
    tokens_ref,
    d_out_ref,
    count_ref,
    order_ref,
    w_qkv_hbm,
    w_out_hbm,
    d_tokens_ref,
    final_ref,
    w_qkv_ref,
    w_out_ref,
    got_tokens,
    got_d_out,
    results,
    joined,
    head_grad,
    attended,
    qkv_grad,
    grad,
    probs_ref,
    live_ref,
    mask_ref,
    pair_sent,
    pair_got,
    dp_sent,
    dp_got,
    held,
    chip_sent,
    chip_got,
    weight_sems,
    tokens_send,
    tokens_recv,
    d_out_send,
    d_out_recv,
    back_send,
    back_recv,
    pair_sems,
    dp_send,
    dp_recv,
    chip_send,
    chip_recv,
):
    rows, width = attended.shape
    steps, slot_count, group, _ = got_tokens.shape
    slots = tokens_ref.shape[0]
    stripe = steps * group
    chips = seq_size // 2
    row_block, column_block = final_ref.shape
    me = lax.axis_index("seq")
    my_dp = lax.axis_index("dp")
    core = lax.rem(me, 2)
    chip = me // 2
    half = seq_size // 2
    far = tuple(reversed(range(half, seq_size)))
    near = tuple(reversed(range(1, half)))
    staggered = tuple(
        first + core * (second - first) for first, second in zip(far + near, near + far)
    )

    def peer(k):
        return me ^ k

    def dp_peer(k):
        return lax.rem(my_dp + k, dp_size)

    barrier = pltpu.get_barrier_semaphore()
    for k in range(1, seq_size):
        pl.semaphore_signal(
            barrier,
            inc=1,
            device_id={"seq": peer(k)},
            device_id_type=pl.DeviceIdType.MESH,
        )
    for k in range(1, dp_size):
        pl.semaphore_signal(
            barrier,
            inc=1,
            device_id={"dp": dp_peer(k)},
            device_id_type=pl.DeviceIdType.MESH,
        )
    pl.semaphore_wait(barrier, seq_size - 1 + dp_size - 1)

    def remote(source, target, send, recv, device):
        return pltpu.make_async_remote_copy(
            src_ref=source,
            dst_ref=target,
            send_sem=send,
            recv_sem=recv,
            device_id=device,
            device_id_type=pl.DeviceIdType.MESH,
        )

    def home(ref, owner, g):
        return ref.at[:, pl.ds(pl.multiple_of(owner * stripe + g * group, group), group), :]

    def away(ref, owner, g):
        return ref.at[g, pl.ds(owner * slots, slots)]

    def spread(source, target, send, recv, g, k):
        return remote(
            home(source, peer(k), g),
            away(target, me, g),
            send.at[g, k],
            recv.at[g, k],
            {"seq": peer(k)},
        )

    def keep_own(source, target, recv, g):
        return pltpu.make_async_copy(home(source, me, g), away(target, me, g), recv.at[g, 0])

    def back(g, k):
        return remote(
            away(results, peer(k), g),
            home(d_tokens_ref, me, g),
            back_send.at[g, k],
            back_recv.at[g, k],
            {"seq": peer(k)},
        )

    def back_own(g):
        return pltpu.make_async_copy(
            away(results, me, g), home(d_tokens_ref, me, g), back_recv.at[g, 0]
        )

    moved = (
        (tokens_ref, got_tokens, tokens_send, tokens_recv),
        (d_out_ref, got_d_out, d_out_send, d_out_recv),
    )

    def depart(which, g):
        source, target, send, recv = moved[which]
        for k in staggered:
            spread(source, target, send, recv, g, k).start()
        keep_own(source, target, recv, g).start()

    def arrived(which, g):
        source, target, send, recv = moved[which]
        for k in range(1, seq_size):
            spread(source, target, send, recv, g, k).wait_recv()
        keep_own(source, target, recv, g).wait()

    def give_back(g):
        for k in staggered:
            back(g, k).start()
        back_own(g).start()

    for at in range(min(AHEAD, 2 * steps)):
        depart(at % 2, at // 2)
    weights = (
        pltpu.make_async_copy(w_qkv_hbm, w_qkv_ref, weight_sems.at[0]),
        pltpu.make_async_copy(w_out_hbm, w_out_ref, weight_sems.at[1]),
    )
    for copy in weights:
        copy.start()
    live_ref[...], mask_ref[...] = mask_in_kernel(group, order_ref[...], count_ref[0])
    grad[...] = jnp.zeros_like(grad)
    for copy in weights:
        copy.wait()

    def depart_next(which, g):
        at = AHEAD + which
        later = g + at // 2

        @pl.when(later < steps)
        def _():
            depart(at % 2, later)

    def pair_copy():
        return remote(
            pair_sent, pair_got, pair_sems.at[0], pair_sems.at[1], {"seq": chip * 2 + 1 - core}
        )

    def row_piece(at, parity):
        start = pl.multiple_of((at * 2 + parity) * row_block, row_block)
        return grad[pl.ds(start, row_block), :]

    def pieces_of(value, d):
        start = 0
        for tile in fold_piece(value[:, d * column_block : (d + 1) * column_block]):
            yield slice(start, start + tile.shape[0]), tile
            start += tile.shape[0]

    def dp_copy(k):
        return remote(
            dp_sent.at[dp_peer(k)],
            dp_got.at[k - 1],
            dp_send.at[k - 1],
            dp_recv.at[k - 1],
            {"dp": dp_peer(k)},
        )

    @pl.loop(0, steps)
    def _(g):
        arrived(0, g)
        depart_next(0, g)
        values = got_tokens[g].astype(jnp.float32).reshape(rows, width)
        center = values - jnp.mean(values, axis=-1, keepdims=True)
        inverse = lax.rsqrt(jnp.mean(center * center, axis=-1, keepdims=True) + 1e-06)
        normalized = center * inverse
        joined[...] = dot(normalized.astype(jnp.bfloat16), w_qkv_ref[...]).astype(jnp.bfloat16)
        attend_forward(joined, mask_ref[...], attended, probs_ref, width, score_scale)

        @pl.when(g == steps - 1)
        def _():
            for earlier in range(max(steps - 3, 0)):
                give_back(earlier)

        arrived(1, g)
        depart_next(1, g)
        masked_wide = got_d_out[g].astype(jnp.float32).reshape(rows, width) * live_ref[...]
        masked = masked_wide.astype(jnp.bfloat16)
        grad[...] += dot(attended[...], masked, TN)

        @pl.when(g == steps - 1)
        def _():
            @pl.loop(0, chips)
            def _(at):
                value = row_piece(at, 1 - core)
                for d in range(dp_size):
                    for where, tile in pieces_of(value, d):
                        pair_sent[d, at, where] = tile.astype(jnp.bfloat16)

            pair_copy().start()

        head_grad[...] = dot(masked, w_out_ref[...], NT).astype(jnp.bfloat16)

        @pl.when(g == steps - 1)
        def _():
            pair_copy().wait_recv()

            @pl.loop(0, chips)
            def _(at):
                value = row_piece(at, core)
                for d in range(dp_size):
                    for where, tile in pieces_of(value, d):
                        total = tile + pair_got[d, at, where].astype(jnp.float32)
                        dp_sent[d, at, where] = total.astype(jnp.bfloat16)

            for k in range(1, dp_size):
                dp_copy(k).start()

            for earlier in range(max(steps - 3, 0), steps - 1):
                give_back(earlier)

        attend_backward(joined, head_grad, probs_ref, qkv_grad, width, score_scale)
        normed_grad = dot(qkv_grad[...], w_qkv_ref[...], NT)
        mean_grad = jnp.mean(normed_grad, axis=-1, keepdims=True)
        mean_cross = jnp.mean(normed_grad * normalized, axis=-1, keepdims=True)
        result = masked_wide + inverse * (normed_grad - mean_grad - normalized * mean_cross)
        results[g] = result.reshape(slot_count, group, width).astype(jnp.bfloat16)

    give_back(steps - 1)
    for k in range(1, dp_size):
        dp_copy(k).wait_recv()

    @pl.loop(0, chips)
    def _(at):
        total = dp_sent[my_dp, at].astype(jnp.float32)
        for k in range(1, dp_size):
            total = total + dp_got[k - 1, at].astype(jnp.float32)
        held[at] = total

    def chip_copy(level):
        return remote(
            chip_sent.at[pl.ds(chips - 2 * (chips >> (level + 1)), chips >> (level + 1))],
            chip_got.at[pl.ds(chips - 2 * (chips >> (level + 1)), chips >> (level + 1))],
            chip_send.at[level],
            chip_recv.at[level],
            {"seq": (chip ^ (1 << level)) * 2 + core},
        )

    for level in range(chips.bit_length() - 1):
        left = chips >> (level + 1)
        base = chips - 2 * left
        bit = lax.rem(chip // (1 << level), 2)
        for at in range(left):
            chip_sent[base + at] = held[2 * at + 1 - bit].astype(jnp.bfloat16)
        chip_copy(level).start()
        chip_copy(level).wait_recv()
        for at in range(left):
            held[at] = held[2 * at + bit] + chip_got[base + at].astype(jnp.float32)
    unfold_piece(held[0], final_ref)

    pair_copy().wait_send()
    for k in range(1, dp_size):
        dp_copy(k).wait_send()
    for level in range(chips.bit_length() - 1):
        chip_copy(level).wait_send()

    @pl.loop(0, steps)
    def _(g):
        for source, target, send, recv in moved:
            for k in range(1, seq_size):
                spread(source, target, send, recv, g, k).wait_send()
        for k in range(1, seq_size):
            back(g, k).wait()
        back_own(g).wait()


def exchange_part(tokens, d_out, frames, frame_order, w_qkv, w_out, slots, seq_size, dp_size):
    row_count, width = tokens.shape
    slot_count = frame_order.shape[1]
    stripe = row_count // slot_count
    steps = stripe // GROUP
    rows = slot_count * GROUP
    chips = seq_size // 2
    levels = chips.bit_length() - 1
    tokens = tokens.reshape(slots, row_count // slots, width)
    d_out = d_out.reshape(tokens.shape)
    any_space = pl.BlockSpec(memory_space=pl.ANY)
    vmem = pl.BlockSpec(memory_space=pltpu.VMEM)
    smem = pl.BlockSpec(memory_space=pltpu.SMEM)
    narrow = jnp.bfloat16
    share = (width // seq_size, width // dp_size)
    parts = (chips, folded_rows(*share), LANES)
    crossing = pltpu.SemaphoreType.DMA((steps, seq_size))
    d_tokens, final = pl.pallas_call(
        functools.partial(exchange_kernel, 1.0 / math.sqrt(width // H), seq_size, dp_size),
        in_specs=[any_space, any_space, smem, vmem, any_space, any_space],
        out_specs=[any_space, vmem],
        out_shape=[
            jax.ShapeDtypeStruct(tokens.shape, narrow),
            jax.ShapeDtypeStruct(share, jnp.float32),
        ],
        scratch_shapes=[
            pltpu.VMEM(w_qkv.shape, narrow),
            pltpu.VMEM(w_out.shape, narrow),
            pltpu.VMEM((steps, slot_count, GROUP, width), narrow),
            pltpu.VMEM((steps, slot_count, GROUP, width), narrow),
            pltpu.VMEM((steps, slot_count, GROUP, width), narrow),
            pltpu.VMEM((rows, 3 * width), narrow),
            pltpu.VMEM((rows, width), narrow),
            pltpu.VMEM((rows, width), narrow),
            pltpu.VMEM((rows, 3 * width), narrow),
            pltpu.VMEM((width, width), jnp.float32),
            pltpu.VMEM((H, rows, rows), jnp.float32),
            pltpu.VMEM((rows, 1), jnp.float32),
            pltpu.VMEM((rows, rows), jnp.float32),
            pltpu.VMEM((dp_size, *parts), narrow),
            pltpu.VMEM((dp_size, *parts), narrow),
            pltpu.VMEM((dp_size, *parts), narrow),
            pltpu.VMEM((dp_size - 1, *parts), narrow),
            pltpu.VMEM(parts, jnp.float32),
            pltpu.VMEM((chips - 1, *parts[1:]), narrow),
            pltpu.VMEM((chips - 1, *parts[1:]), narrow),
            pltpu.SemaphoreType.DMA((2,)),
            crossing,
            crossing,
            crossing,
            crossing,
            crossing,
            crossing,
            pltpu.SemaphoreType.DMA((2,)),
            pltpu.SemaphoreType.DMA((dp_size - 1,)),
            pltpu.SemaphoreType.DMA((dp_size - 1,)),
            pltpu.SemaphoreType.DMA((levels,)),
            pltpu.SemaphoreType.DMA((levels,)),
        ],
        compiler_params=pltpu.CompilerParams(
            collective_id=0, has_side_effects=True, vmem_limit_bytes=VMEM_BYTES
        ),
    )(tokens, d_out, frames, frame_order, w_qkv, w_out)
    return d_tokens, final


def body(tokens, d_out, frames, frame_order, w_qkv, w_out):
    _, row_count, width = tokens.shape
    seq_size = lax.axis_size("seq")
    slot_count = frame_order.shape[1]
    stripe = row_count // slot_count
    patch_count = row_count * seq_size // slot_count
    slots = max(1, row_count // patch_count)
    piece = row_count // slots // seq_size
    live_slots = (frame_order[0] < frames[0]).astype(jnp.float32)

    dp_size = lax.axis_size("dp")
    if (
        piece == stripe
        and stripe % GROUP == 0
        and seq_size & (seq_size - 1) == 0
        and seq_size > 2
        and dp_size > 1
        and width % (16 * seq_size) == 0
    ):
        d_rows, final_out = exchange_part(
            tokens[0], d_out[0], frames, frame_order, w_qkv, w_out, slots, seq_size, dp_size
        )
        return (d_rows.reshape(tokens.shape), final_out)

    def spread(rows):
        sent = rows.reshape(slots, seq_size, piece, width)
        got = lax.all_to_all(sent, "seq", split_axis=1, concat_axis=0, tiled=True)
        return got.reshape(slot_count, stripe, width)

    d_rows, grad_out = local_part(spread(tokens), spread(d_out), live_slots, w_qkv, w_out)
    back = d_rows.reshape(seq_size * slots, 1, piece, width)
    d_tokens = lax.all_to_all(back, "seq", split_axis=0, concat_axis=1, tiled=True)
    share = lax.psum_scatter(
        grad_out.astype(jnp.bfloat16), "dp", scatter_dimension=1, tiled=True
    ).astype(jnp.float32)
    final_out = lax.psum_scatter(share, "seq", scatter_dimension=0, tiled=True)
    return (d_tokens.reshape(tokens.shape), final_out)


def solution(mesh):
    placed = (P("dp", "seq", None), P("dp", "seq", None), P("dp"), P("dp", None), P(), P())
    return jax.shard_map(
        body,
        mesh=mesh,
        in_specs=placed,
        out_specs=(P("dp", "seq", None), P("seq", "dp")),
        check_vma=False,
    )
```

```python
import functools
import math

import jax
import jax.numpy as jnp
from jax import lax
from jax.experimental import pallas as pl
from jax.experimental.pallas import tpu as pltpu
from jax.sharding import PartitionSpec as P

H = 16
LANES = 128
GROUP = 8
AHEAD = 3
VMEM_BYTES = 50 * 2**20
SUBLANES = 16
NT = (((1,), (1,)), ((), ()))
TN = (((0,), (0,)), ((), ()))


def dot(a, b, dims=(((1,), (0,)), ((), ()))):
    return lax.dot_general(a, b, dims, preferred_element_type=jnp.float32)


def attend(joined, head_grad, mask, attended, qkv_grad, width, score_scale):
    head_dim = width // H
    column = lax.broadcasted_iota(jnp.int32, (1, 2 * LANES), 1)
    pending = [{}, {}, {}, {}]
    for h in range(H):
        low, high = h * head_dim, (h + 1) * head_dim
        first, last = low // LANES, -(-high // LANES)
        start, size = first * LANES, (last - first) * LANES
        keep = jnp.where(
            (column[:, :size] >= low - start) & (column[:, :size] < high - start), 1.0, 0.0
        ).astype(jnp.bfloat16)
        q = joined[:, start : start + size] * keep
        k = joined[:, width + start : width + start + size] * keep
        v = joined[:, 2 * width + start : 2 * width + start + size] * keep
        g = head_grad[:, start : start + size] * keep
        scores = dot(q, k, NT) * score_scale + mask
        exponent = jnp.exp(scores - jnp.max(scores, axis=-1, keepdims=True))
        probs = exponent * (1.0 / jnp.sum(exponent, axis=-1, keepdims=True))
        rounded = probs.astype(jnp.bfloat16)
        prob_grad = dot(g, v, NT)
        inner = jnp.sum(probs * prob_grad, axis=-1, keepdims=True)
        score_grad = (probs * (prob_grad - inner) * score_scale).astype(jnp.bfloat16)
        results = (
            dot(rounded, v),
            dot(score_grad, k),
            dot(score_grad, q, TN),
            dot(rounded, g, TN),
        )
        for which, result in enumerate(results):
            for tile in range(first, last):
                piece = result[:, (tile - first) * LANES : (tile - first + 1) * LANES]
                held = pending[which].pop(tile, None)
                piece = piece if held is None else held + piece
                if (tile + 1) * LANES <= high:
                    piece = piece.astype(jnp.bfloat16)
                    if which == 0:
                        attended[:, tile * LANES : (tile + 1) * LANES] = piece
                    else:
                        at = (which - 1) * width + tile * LANES
                        qkv_grad[:, at : at + LANES] = piece
                else:
                    pending[which][tile] = piece


def kernel(
    score_scale,
    tokens_ref,
    d_out_ref,
    live_ref,
    mask_ref,
    w_qkv_ref,
    w_out_ref,
    d_tokens_ref,
    grad_ref,
    joined,
    head_grad,
    attended,
    qkv_grad,
):
    rows, width = attended.shape
    values = tokens_ref[...].astype(jnp.float32).reshape(rows, width)
    center = values - jnp.mean(values, axis=-1, keepdims=True)
    inverse = lax.rsqrt(jnp.mean(center * center, axis=-1, keepdims=True) + 1e-06)
    normalized = center * inverse
    normed = normalized.astype(jnp.bfloat16)
    masked_wide = d_out_ref[...].astype(jnp.float32).reshape(rows, width) * live_ref[...]
    masked = masked_wide.astype(jnp.bfloat16)
    joined[...] = dot(normed, w_qkv_ref[...]).astype(jnp.bfloat16)
    head_grad[...] = dot(masked, w_out_ref[...], NT).astype(jnp.bfloat16)
    attend(joined, head_grad, mask_ref[...], attended, qkv_grad, width, score_scale)
    term = dot(attended[...], masked, TN)

    @pl.when(pl.program_id(0) == 0)
    def _():
        grad_ref[...] = term

    @pl.when(pl.program_id(0) != 0)
    def _():
        grad_ref[...] += term

    normed_grad = dot(qkv_grad[...], w_qkv_ref[...], NT)
    mean_grad = jnp.mean(normed_grad, axis=-1, keepdims=True)
    mean_cross = jnp.mean(normed_grad * normalized, axis=-1, keepdims=True)
    result = masked_wide + inverse * (normed_grad - mean_grad - normalized * mean_cross)
    d_tokens_ref[...] = result.reshape(d_tokens_ref.shape).astype(jnp.bfloat16)


def mask_of(live_slots, rows, group):
    at = jnp.arange(rows, dtype=jnp.int32)
    live_rows = jnp.repeat(live_slots, group)
    mask = jnp.where(
        (at[:, None] % group == at[None, :] % group) & (live_rows[None, :] > 0.5), 0.0, -1e30
    ).astype(jnp.float32)
    return live_rows, mask


def local_part(tokens, d_out, live_slots, w_qkv, w_out):
    slot_count, stripe, width = tokens.shape
    group = min(GROUP, stripe)
    rows = slot_count * group
    steps = stripe // group
    live_rows, mask = mask_of(live_slots, rows, group)
    if steps == 1:
        tokens, d_out = tokens.reshape(rows, width), d_out.reshape(rows, width)
        moving = pl.BlockSpec((rows, width), lambda i: (0, 0))
    else:
        moving = pl.BlockSpec((slot_count, group, width), lambda i: (0, i, 0))

    def whole(shape):
        return pl.BlockSpec(shape, lambda i: (0, 0), pipeline_mode=pl.Buffered(1))

    d_tokens, grad = pl.pallas_call(
        functools.partial(kernel, 1.0 / math.sqrt(width // H)),
        grid=(steps,),
        in_specs=[
            moving,
            moving,
            whole((rows, 1)),
            whole((rows, rows)),
            whole(w_qkv.shape),
            whole(w_out.shape),
        ],
        out_specs=[moving, whole((width, width))],
        out_shape=[
            jax.ShapeDtypeStruct(tokens.shape, jnp.bfloat16),
            jax.ShapeDtypeStruct((width, width), jnp.float32),
        ],
        scratch_shapes=[
            pltpu.VMEM((rows, 3 * width), jnp.bfloat16),
            pltpu.VMEM((rows, width), jnp.bfloat16),
            pltpu.VMEM((rows, width), jnp.bfloat16),
            pltpu.VMEM((rows, 3 * width), jnp.bfloat16),
        ],
        compiler_params=pltpu.CompilerParams(
            dimension_semantics=("arbitrary",), vmem_limit_bytes=60 * 2**20
        ),
    )(tokens, d_out, live_rows[:, None], mask, w_qkv, w_out)
    return d_tokens.reshape(slot_count, stripe, width), grad


def mask_in_kernel(group, order, count):
    rows = order.shape[1] * group
    live = (order < count).astype(jnp.float32)
    slot_of = lax.broadcasted_iota(jnp.int32, (rows, order.shape[1]), 1) * group
    row_of = lax.broadcasted_iota(jnp.int32, slot_of.shape, 0)
    owns = (row_of >= slot_of) & (row_of < slot_of + group)
    live_rows = jnp.sum(jnp.where(owns, live, 0.0), axis=-1, keepdims=True)
    live_columns = dot(jnp.broadcast_to(live, (8, order.shape[1])), owns.astype(jnp.float32), NT)
    row = lax.broadcasted_iota(jnp.int32, (rows, rows), 0)
    column = lax.broadcasted_iota(jnp.int32, (rows, rows), 1)
    same = lax.rem(row, group) == lax.rem(column, group)
    mask = jnp.where(same & (live_columns[:1] > 0.5), 0.0, -1e30)
    return live_rows, mask


def head_window(width, h):
    head_dim = width // H
    low, high = h * head_dim, (h + 1) * head_dim
    first, last = low // LANES, -(-high // LANES)
    start, size = first * LANES, (last - first) * LANES
    column = lax.broadcasted_iota(jnp.int32, (1, 2 * LANES), 1)
    keep = jnp.where(
        (column[:, :size] >= low - start) & (column[:, :size] < high - start), 1.0, 0.0
    ).astype(jnp.bfloat16)
    return start, size, high, keep


def put_head(pending, result, start, size, high, target, offset):
    for tile in range(start // LANES, (start + size) // LANES):
        piece = result[:, tile * LANES - start : (tile + 1) * LANES - start]
        held = pending.pop(tile, None)
        piece = piece if held is None else held + piece
        if (tile + 1) * LANES <= high:
            at = offset + tile * LANES
            target[:, at : at + LANES] = piece.astype(jnp.bfloat16)
        else:
            pending[tile] = piece


def attend_forward(joined, mask, attended, probs_ref, width, score_scale):
    pending = {}
    for h in range(H):
        start, size, high, keep = head_window(width, h)
        q = joined[:, start : start + size] * keep
        k = joined[:, width + start : width + start + size]
        v = joined[:, 2 * width + start : 2 * width + start + size] * keep
        scores = dot(q, k, NT) * score_scale + mask
        exponent = jnp.exp(scores - jnp.max(scores, axis=-1, keepdims=True))
        probs = exponent * (1.0 / jnp.sum(exponent, axis=-1, keepdims=True))
        probs_ref[h] = probs
        result = dot(probs.astype(jnp.bfloat16), v)
        put_head(pending, result, start, size, high, attended, 0)


def attend_backward(joined, head_grad, probs_ref, qkv_grad, width, score_scale):
    pending = [{}, {}, {}]
    for h in range(H):
        start, size, high, keep = head_window(width, h)
        q = joined[:, start : start + size] * keep
        k = joined[:, width + start : width + start + size] * keep
        v = joined[:, 2 * width + start : 2 * width + start + size]
        g = head_grad[:, start : start + size] * keep
        probs = probs_ref[h]
        prob_grad = dot(g, v, NT)
        inner = jnp.sum(probs * prob_grad, axis=-1, keepdims=True)
        score_grad = (probs * (prob_grad - inner) * score_scale).astype(jnp.bfloat16)
        results = (
            dot(score_grad, k),
            dot(score_grad, q, TN),
            dot(probs.astype(jnp.bfloat16), g, TN),
        )
        for which, result in enumerate(results):
            put_head(pending[which], result, start, size, high, qkv_grad, which * width)


def fold_of(row_block, column_block):
    rest = column_block % LANES
    fits = [f for f in range(1, LANES // max(rest, 1) + 1) if row_block % (f * SUBLANES) == 0]
    return column_block // LANES, rest, fits[-1] if fits else 1


def folded_rows(row_block, column_block):
    full, rest, fold = fold_of(row_block, column_block)
    return full * row_block + (row_block // fold if rest else 0)


def fold_piece(value):
    full, rest, fold = fold_of(*value.shape)
    tiles = [value[:, t * LANES : (t + 1) * LANES] for t in range(full)]
    if rest:
        size = value.shape[0] // fold
        parts = [value[f * size : (f + 1) * size, full * LANES :] for f in range(fold)]
        if rest * fold < LANES:
            parts.append(jnp.zeros((size, LANES - rest * fold), value.dtype))
        tiles.append(jnp.concatenate(parts, axis=1))
    return tiles


def unfold_piece(value, target):
    row_block, column_block = target.shape
    full, rest, fold = fold_of(row_block, column_block)
    for t in range(full):
        target[:, t * LANES : (t + 1) * LANES] = value[t * row_block : (t + 1) * row_block]
    if rest:
        size = row_block // fold
        tail = value[full * row_block :]
        for f in range(fold):
            target[f * size : (f + 1) * size, full * LANES :] = tail[:, f * rest : (f + 1) * rest]


def exchange_kernel(
    score_scale,
    seq_size,
    dp_size,
    tokens_ref,
    d_out_ref,
    count_ref,
    order_ref,
    w_qkv_hbm,
    w_out_hbm,
    d_tokens_ref,
    final_ref,
    w_qkv_ref,
    w_out_ref,
    got_tokens,
    got_d_out,
    results,
    joined,
    head_grad,
    attended,
    qkv_grad,
    grad,
    probs_ref,
    live_ref,
    mask_ref,
    pair_sent,
    pair_got,
    dp_sent,
    dp_got,
    held,
    chip_sent,
    chip_got,
    weight_sems,
    tokens_send,
    tokens_recv,
    d_out_send,
    d_out_recv,
    back_send,
    back_recv,
    pair_sems,
    dp_send,
    dp_recv,
    chip_send,
    chip_recv,
):
    rows, width = attended.shape
    steps, slot_count, group, _ = got_tokens.shape
    slots = tokens_ref.shape[0]
    stripe = steps * group
    chips = seq_size // 2
    row_block, column_block = final_ref.shape
    me = lax.axis_index("seq")
    my_dp = lax.axis_index("dp")
    core = lax.rem(me, 2)
    chip = me // 2
    half = seq_size // 2
    far = tuple(reversed(range(half, seq_size)))
    near = tuple(reversed(range(1, half)))
    outer, inner = far[: half // 2], far[half // 2 :]
    staggered = tuple(
        first + core * (second - first) for first, second in zip(far + near, outer + near + inner)
    )

    def peer(k):
        return me ^ k

    def dp_peer(k):
        return lax.rem(my_dp + k, dp_size)

    barrier = pltpu.get_barrier_semaphore()
    for k in range(1, seq_size):
        pl.semaphore_signal(
            barrier,
            inc=1,
            device_id={"seq": peer(k)},
            device_id_type=pl.DeviceIdType.MESH,
        )
    for k in range(1, dp_size):
        pl.semaphore_signal(
            barrier,
            inc=1,
            device_id={"dp": dp_peer(k)},
            device_id_type=pl.DeviceIdType.MESH,
        )
    pl.semaphore_wait(barrier, seq_size - 1 + dp_size - 1)

    def remote(source, target, send, recv, device):
        return pltpu.make_async_remote_copy(
            src_ref=source,
            dst_ref=target,
            send_sem=send,
            recv_sem=recv,
            device_id=device,
            device_id_type=pl.DeviceIdType.MESH,
        )

    def home(ref, owner, g):
        return ref.at[:, pl.ds(pl.multiple_of(owner * stripe + g * group, group), group), :]

    def away(ref, owner, g):
        return ref.at[g, pl.ds(owner * slots, slots)]

    def spread(source, target, send, recv, g, k):
        return remote(
            home(source, peer(k), g),
            away(target, me, g),
            send.at[g, k],
            recv.at[g, k],
            {"seq": peer(k)},
        )

    def keep_own(source, target, recv, g):
        return pltpu.make_async_copy(home(source, me, g), away(target, me, g), recv.at[g, 0])

    def back(g, k):
        return remote(
            away(results, peer(k), g),
            home(d_tokens_ref, me, g),
            back_send.at[g, k],
            back_recv.at[g, k],
            {"seq": peer(k)},
        )

    def back_own(g):
        return pltpu.make_async_copy(
            away(results, me, g), home(d_tokens_ref, me, g), back_recv.at[g, 0]
        )

    moved = (
        (tokens_ref, got_tokens, tokens_send, tokens_recv),
        (d_out_ref, got_d_out, d_out_send, d_out_recv),
    )

    def depart(which, g):
        source, target, send, recv = moved[which]
        for k in staggered:
            spread(source, target, send, recv, g, k).start()
        keep_own(source, target, recv, g).start()

    def arrived(which, g):
        source, target, send, recv = moved[which]
        for k in range(1, seq_size):
            spread(source, target, send, recv, g, k).wait_recv()
        keep_own(source, target, recv, g).wait()

    def give_back(g):
        for k in staggered:
            back(g, k).start()
        back_own(g).start()

    for at in range(min(AHEAD, 2 * steps)):
        depart(at % 2, at // 2)
    weights = (
        pltpu.make_async_copy(w_qkv_hbm, w_qkv_ref, weight_sems.at[0]),
        pltpu.make_async_copy(w_out_hbm, w_out_ref, weight_sems.at[1]),
    )
    for copy in weights:
        copy.start()
    live_ref[...], mask_ref[...] = mask_in_kernel(group, order_ref[...], count_ref[0])
    grad[...] = jnp.zeros_like(grad)
    for copy in weights:
        copy.wait()

    def depart_next(which, g):
        at = AHEAD + which
        later = g + at // 2

        @pl.when(later < steps)
        def _():
            depart(at % 2, later)

    def pair_copy():
        return remote(
            pair_sent, pair_got, pair_sems.at[0], pair_sems.at[1], {"seq": chip * 2 + 1 - core}
        )

    def row_piece(at, parity):
        start = pl.multiple_of((at * 2 + parity) * row_block, row_block)
        return grad[pl.ds(start, row_block), :]

    def pieces_of(value, d):
        start = 0
        for tile in fold_piece(value[:, d * column_block : (d + 1) * column_block]):
            yield slice(start, start + tile.shape[0]), tile
            start += tile.shape[0]

    def dp_copy(k):
        return remote(
            dp_sent.at[dp_peer(k)],
            dp_got.at[k - 1],
            dp_send.at[k - 1],
            dp_recv.at[k - 1],
            {"dp": dp_peer(k)},
        )

    @pl.loop(0, steps)
    def _(g):
        arrived(0, g)
        depart_next(0, g)
        values = got_tokens[g].astype(jnp.float32).reshape(rows, width)
        center = values - jnp.mean(values, axis=-1, keepdims=True)
        inverse = lax.rsqrt(jnp.mean(center * center, axis=-1, keepdims=True) + 1e-06)
        normalized = center * inverse
        joined[...] = dot(normalized.astype(jnp.bfloat16), w_qkv_ref[...]).astype(jnp.bfloat16)
        attend_forward(joined, mask_ref[...], attended, probs_ref, width, score_scale)

        @pl.when(g == steps - 1)
        def _():
            for earlier in range(max(steps - 3, 0)):
                give_back(earlier)

        arrived(1, g)
        depart_next(1, g)
        masked_wide = got_d_out[g].astype(jnp.float32).reshape(rows, width) * live_ref[...]
        masked = masked_wide.astype(jnp.bfloat16)
        grad[...] += dot(attended[...], masked, TN)

        @pl.when(g == steps - 1)
        def _():
            @pl.loop(0, chips)
            def _(at):
                value = row_piece(at, 1 - core)
                for d in range(dp_size):
                    for where, tile in pieces_of(value, d):
                        pair_sent[d, at, where] = tile.astype(jnp.bfloat16)

            pair_copy().start()

        head_grad[...] = dot(masked, w_out_ref[...], NT).astype(jnp.bfloat16)

        @pl.when(g == steps - 1)
        def _():
            pair_copy().wait_recv()

            @pl.loop(0, chips)
            def _(at):
                value = row_piece(at, core)
                for d in range(dp_size):
                    for where, tile in pieces_of(value, d):
                        total = tile + pair_got[d, at, where].astype(jnp.float32)
                        dp_sent[d, at, where] = total.astype(jnp.bfloat16)

            for k in range(1, dp_size):
                dp_copy(k).start()

            for earlier in range(max(steps - 3, 0), steps - 1):
                give_back(earlier)

        attend_backward(joined, head_grad, probs_ref, qkv_grad, width, score_scale)
        normed_grad = dot(qkv_grad[...], w_qkv_ref[...], NT)
        mean_grad = jnp.mean(normed_grad, axis=-1, keepdims=True)
        mean_cross = jnp.mean(normed_grad * normalized, axis=-1, keepdims=True)
        result = masked_wide + inverse * (normed_grad - mean_grad - normalized * mean_cross)
        results[g] = result.reshape(slot_count, group, width).astype(jnp.bfloat16)

    for k in range(1, dp_size):
        dp_copy(k).wait_recv()

    @pl.loop(0, chips)
    def _(at):
        total = dp_sent[my_dp, at].astype(jnp.float32)
        for k in range(1, dp_size):
            total = total + dp_got[k - 1, at].astype(jnp.float32)
        held[at] = total

    def chip_copy(level):
        return remote(
            chip_sent.at[pl.ds(chips - 2 * (chips >> (level + 1)), chips >> (level + 1))],
            chip_got.at[pl.ds(chips - 2 * (chips >> (level + 1)), chips >> (level + 1))],
            chip_send.at[level],
            chip_recv.at[level],
            {"seq": (chip ^ (1 << level)) * 2 + core},
        )

    for level in range(chips.bit_length() - 1):
        left = chips >> (level + 1)
        base = chips - 2 * left
        bit = lax.rem(chip // (1 << level), 2)
        for at in range(left):
            chip_sent[base + at] = held[2 * at + 1 - bit].astype(jnp.bfloat16)
        chip_copy(level).start()
        if level == 0:
            give_back(steps - 1)
        chip_copy(level).wait_recv()
        for at in range(left):
            held[at] = held[2 * at + bit] + chip_got[base + at].astype(jnp.float32)
    unfold_piece(held[0], final_ref)

    pair_copy().wait_send()
    for k in range(1, dp_size):
        dp_copy(k).wait_send()
    for level in range(chips.bit_length() - 1):
        chip_copy(level).wait_send()

    @pl.loop(0, steps)
    def _(g):
        for source, target, send, recv in moved:
            for k in range(1, seq_size):
                spread(source, target, send, recv, g, k).wait_send()
        for k in range(1, seq_size):
            back(g, k).wait()
        back_own(g).wait()


def exchange_part(tokens, d_out, frames, frame_order, w_qkv, w_out, slots, seq_size, dp_size):
    row_count, width = tokens.shape
    slot_count = frame_order.shape[1]
    stripe = row_count // slot_count
    steps = stripe // GROUP
    rows = slot_count * GROUP
    chips = seq_size // 2
    levels = chips.bit_length() - 1
    tokens = tokens.reshape(slots, row_count // slots, width)
    d_out = d_out.reshape(tokens.shape)
    any_space = pl.BlockSpec(memory_space=pl.ANY)
    vmem = pl.BlockSpec(memory_space=pltpu.VMEM)
    smem = pl.BlockSpec(memory_space=pltpu.SMEM)
    narrow = jnp.bfloat16
    share = (width // seq_size, width // dp_size)
    parts = (chips, folded_rows(*share), LANES)
    crossing = pltpu.SemaphoreType.DMA((steps, seq_size))
    d_tokens, final = pl.pallas_call(
        functools.partial(exchange_kernel, 1.0 / math.sqrt(width // H), seq_size, dp_size),
        in_specs=[any_space, any_space, smem, vmem, any_space, any_space],
        out_specs=[any_space, vmem],
        out_shape=[
            jax.ShapeDtypeStruct(tokens.shape, narrow),
            jax.ShapeDtypeStruct(share, jnp.float32),
        ],
        scratch_shapes=[
            pltpu.VMEM(w_qkv.shape, narrow),
            pltpu.VMEM(w_out.shape, narrow),
            pltpu.VMEM((steps, slot_count, GROUP, width), narrow),
            pltpu.VMEM((steps, slot_count, GROUP, width), narrow),
            pltpu.VMEM((steps, slot_count, GROUP, width), narrow),
            pltpu.VMEM((rows, 3 * width), narrow),
            pltpu.VMEM((rows, width), narrow),
            pltpu.VMEM((rows, width), narrow),
            pltpu.VMEM((rows, 3 * width), narrow),
            pltpu.VMEM((width, width), jnp.float32),
            pltpu.VMEM((H, rows, rows), jnp.float32),
            pltpu.VMEM((rows, 1), jnp.float32),
            pltpu.VMEM((rows, rows), jnp.float32),
            pltpu.VMEM((dp_size, *parts), narrow),
            pltpu.VMEM((dp_size, *parts), narrow),
            pltpu.VMEM((dp_size, *parts), narrow),
            pltpu.VMEM((dp_size - 1, *parts), narrow),
            pltpu.VMEM(parts, jnp.float32),
            pltpu.VMEM((chips - 1, *parts[1:]), narrow),
            pltpu.VMEM((chips - 1, *parts[1:]), narrow),
            pltpu.SemaphoreType.DMA((2,)),
            crossing,
            crossing,
            crossing,
            crossing,
            crossing,
            crossing,
            pltpu.SemaphoreType.DMA((2,)),
            pltpu.SemaphoreType.DMA((dp_size - 1,)),
            pltpu.SemaphoreType.DMA((dp_size - 1,)),
            pltpu.SemaphoreType.DMA((levels,)),
            pltpu.SemaphoreType.DMA((levels,)),
        ],
        compiler_params=pltpu.CompilerParams(
            collective_id=0, has_side_effects=True, vmem_limit_bytes=VMEM_BYTES
        ),
    )(tokens, d_out, frames, frame_order, w_qkv, w_out)
    return d_tokens, final


def body(tokens, d_out, frames, frame_order, w_qkv, w_out):
    _, row_count, width = tokens.shape
    seq_size = lax.axis_size("seq")
    slot_count = frame_order.shape[1]
    stripe = row_count // slot_count
    patch_count = row_count * seq_size // slot_count
    slots = max(1, row_count // patch_count)
    piece = row_count // slots // seq_size
    live_slots = (frame_order[0] < frames[0]).astype(jnp.float32)

    dp_size = lax.axis_size("dp")
    if (
        piece == stripe
        and stripe % GROUP == 0
        and seq_size & (seq_size - 1) == 0
        and seq_size > 2
        and dp_size > 1
        and width % (16 * seq_size) == 0
    ):
        d_rows, final_out = exchange_part(
            tokens[0], d_out[0], frames, frame_order, w_qkv, w_out, slots, seq_size, dp_size
        )
        return (d_rows.reshape(tokens.shape), final_out)

    def spread(rows):
        sent = rows.reshape(slots, seq_size, piece, width)
        got = lax.all_to_all(sent, "seq", split_axis=1, concat_axis=0, tiled=True)
        return got.reshape(slot_count, stripe, width)

    d_rows, grad_out = local_part(spread(tokens), spread(d_out), live_slots, w_qkv, w_out)
    back = d_rows.reshape(seq_size * slots, 1, piece, width)
    d_tokens = lax.all_to_all(back, "seq", split_axis=0, concat_axis=1, tiled=True)
    share = lax.psum_scatter(
        grad_out.astype(jnp.bfloat16), "dp", scatter_dimension=1, tiled=True
    ).astype(jnp.float32)
    final_out = lax.psum_scatter(share, "seq", scatter_dimension=0, tiled=True)
    return (d_tokens.reshape(tokens.shape), final_out)


def solution(mesh):
    placed = (P("dp", "seq", None), P("dp", "seq", None), P("dp"), P("dp", None), P(), P())
    return jax.shard_map(
        body,
        mesh=mesh,
        in_specs=placed,
        out_specs=(P("dp", "seq", None), P("seq", "dp")),
        check_vma=False,
    )
```

```python
import functools
import math

import jax
import jax.numpy as jnp
from jax import lax
from jax.experimental import pallas as pl
from jax.experimental.pallas import tpu as pltpu
from jax.sharding import PartitionSpec as P

H = 16
LANES = 128
GROUP = 8
AHEAD = 3
VMEM_BYTES = 50 * 2**20
SUBLANES = 16
NT = (((1,), (1,)), ((), ()))
TN = (((0,), (0,)), ((), ()))


def dot(a, b, dims=(((1,), (0,)), ((), ()))):
    return lax.dot_general(a, b, dims, preferred_element_type=jnp.float32)


def attend(joined, head_grad, mask, attended, qkv_grad, width, score_scale):
    head_dim = width // H
    column = lax.broadcasted_iota(jnp.int32, (1, 2 * LANES), 1)
    pending = [{}, {}, {}, {}]
    for h in range(H):
        low, high = h * head_dim, (h + 1) * head_dim
        first, last = low // LANES, -(-high // LANES)
        start, size = first * LANES, (last - first) * LANES
        keep = jnp.where(
            (column[:, :size] >= low - start) & (column[:, :size] < high - start), 1.0, 0.0
        ).astype(jnp.bfloat16)
        q = joined[:, start : start + size] * keep
        k = joined[:, width + start : width + start + size] * keep
        v = joined[:, 2 * width + start : 2 * width + start + size] * keep
        g = head_grad[:, start : start + size] * keep
        scores = dot(q, k, NT) * score_scale + mask
        exponent = jnp.exp(scores - jnp.max(scores, axis=-1, keepdims=True))
        probs = exponent * (1.0 / jnp.sum(exponent, axis=-1, keepdims=True))
        rounded = probs.astype(jnp.bfloat16)
        prob_grad = dot(g, v, NT)
        inner = jnp.sum(probs * prob_grad, axis=-1, keepdims=True)
        score_grad = (probs * (prob_grad - inner) * score_scale).astype(jnp.bfloat16)
        results = (
            dot(rounded, v),
            dot(score_grad, k),
            dot(score_grad, q, TN),
            dot(rounded, g, TN),
        )
        for which, result in enumerate(results):
            for tile in range(first, last):
                piece = result[:, (tile - first) * LANES : (tile - first + 1) * LANES]
                held = pending[which].pop(tile, None)
                piece = piece if held is None else held + piece
                if (tile + 1) * LANES <= high:
                    piece = piece.astype(jnp.bfloat16)
                    if which == 0:
                        attended[:, tile * LANES : (tile + 1) * LANES] = piece
                    else:
                        at = (which - 1) * width + tile * LANES
                        qkv_grad[:, at : at + LANES] = piece
                else:
                    pending[which][tile] = piece


def kernel(
    score_scale,
    tokens_ref,
    d_out_ref,
    live_ref,
    mask_ref,
    w_qkv_ref,
    w_out_ref,
    d_tokens_ref,
    grad_ref,
    joined,
    head_grad,
    attended,
    qkv_grad,
):
    rows, width = attended.shape
    values = tokens_ref[...].astype(jnp.float32).reshape(rows, width)
    center = values - jnp.mean(values, axis=-1, keepdims=True)
    inverse = lax.rsqrt(jnp.mean(center * center, axis=-1, keepdims=True) + 1e-06)
    normalized = center * inverse
    normed = normalized.astype(jnp.bfloat16)
    masked_wide = d_out_ref[...].astype(jnp.float32).reshape(rows, width) * live_ref[...]
    masked = masked_wide.astype(jnp.bfloat16)
    joined[...] = dot(normed, w_qkv_ref[...]).astype(jnp.bfloat16)
    head_grad[...] = dot(masked, w_out_ref[...], NT).astype(jnp.bfloat16)
    attend(joined, head_grad, mask_ref[...], attended, qkv_grad, width, score_scale)
    term = dot(attended[...], masked, TN)

    @pl.when(pl.program_id(0) == 0)
    def _():
        grad_ref[...] = term

    @pl.when(pl.program_id(0) != 0)
    def _():
        grad_ref[...] += term

    normed_grad = dot(qkv_grad[...], w_qkv_ref[...], NT)
    mean_grad = jnp.mean(normed_grad, axis=-1, keepdims=True)
    mean_cross = jnp.mean(normed_grad * normalized, axis=-1, keepdims=True)
    result = masked_wide + inverse * (normed_grad - mean_grad - normalized * mean_cross)
    d_tokens_ref[...] = result.reshape(d_tokens_ref.shape).astype(jnp.bfloat16)


def mask_of(live_slots, rows, group):
    at = jnp.arange(rows, dtype=jnp.int32)
    live_rows = jnp.repeat(live_slots, group)
    mask = jnp.where(
        (at[:, None] % group == at[None, :] % group) & (live_rows[None, :] > 0.5), 0.0, -1e30
    ).astype(jnp.float32)
    return live_rows, mask


def local_part(tokens, d_out, live_slots, w_qkv, w_out):
    slot_count, stripe, width = tokens.shape
    group = min(GROUP, stripe)
    rows = slot_count * group
    steps = stripe // group
    live_rows, mask = mask_of(live_slots, rows, group)
    if steps == 1:
        tokens, d_out = tokens.reshape(rows, width), d_out.reshape(rows, width)
        moving = pl.BlockSpec((rows, width), lambda i: (0, 0))
    else:
        moving = pl.BlockSpec((slot_count, group, width), lambda i: (0, i, 0))

    def whole(shape):
        return pl.BlockSpec(shape, lambda i: (0, 0), pipeline_mode=pl.Buffered(1))

    d_tokens, grad = pl.pallas_call(
        functools.partial(kernel, 1.0 / math.sqrt(width // H)),
        grid=(steps,),
        in_specs=[
            moving,
            moving,
            whole((rows, 1)),
            whole((rows, rows)),
            whole(w_qkv.shape),
            whole(w_out.shape),
        ],
        out_specs=[moving, whole((width, width))],
        out_shape=[
            jax.ShapeDtypeStruct(tokens.shape, jnp.bfloat16),
            jax.ShapeDtypeStruct((width, width), jnp.float32),
        ],
        scratch_shapes=[
            pltpu.VMEM((rows, 3 * width), jnp.bfloat16),
            pltpu.VMEM((rows, width), jnp.bfloat16),
            pltpu.VMEM((rows, width), jnp.bfloat16),
            pltpu.VMEM((rows, 3 * width), jnp.bfloat16),
        ],
        compiler_params=pltpu.CompilerParams(
            dimension_semantics=("arbitrary",), vmem_limit_bytes=60 * 2**20
        ),
    )(tokens, d_out, live_rows[:, None], mask, w_qkv, w_out)
    return d_tokens.reshape(slot_count, stripe, width), grad


def mask_in_kernel(group, order, count):
    rows = order.shape[1] * group
    live = (order < count).astype(jnp.float32)
    slot_of = lax.broadcasted_iota(jnp.int32, (rows, order.shape[1]), 1) * group
    row_of = lax.broadcasted_iota(jnp.int32, slot_of.shape, 0)
    owns = (row_of >= slot_of) & (row_of < slot_of + group)
    live_rows = jnp.sum(jnp.where(owns, live, 0.0), axis=-1, keepdims=True)
    live_columns = dot(jnp.broadcast_to(live, (8, order.shape[1])), owns.astype(jnp.float32), NT)
    row = lax.broadcasted_iota(jnp.int32, (rows, rows), 0)
    column = lax.broadcasted_iota(jnp.int32, (rows, rows), 1)
    same = lax.rem(row, group) == lax.rem(column, group)
    mask = jnp.where(same & (live_columns[:1] > 0.5), 0.0, -1e30)
    return live_rows, mask


def head_window(width, h):
    head_dim = width // H
    low, high = h * head_dim, (h + 1) * head_dim
    first, last = low // LANES, -(-high // LANES)
    start, size = first * LANES, (last - first) * LANES
    column = lax.broadcasted_iota(jnp.int32, (1, 2 * LANES), 1)
    keep = jnp.where(
        (column[:, :size] >= low - start) & (column[:, :size] < high - start), 1.0, 0.0
    ).astype(jnp.bfloat16)
    return start, size, high, keep


def put_head(pending, result, start, size, high, target, offset):
    for tile in range(start // LANES, (start + size) // LANES):
        piece = result[:, tile * LANES - start : (tile + 1) * LANES - start]
        held = pending.pop(tile, None)
        piece = piece if held is None else held + piece
        if (tile + 1) * LANES <= high:
            at = offset + tile * LANES
            target[:, at : at + LANES] = piece.astype(jnp.bfloat16)
        else:
            pending[tile] = piece


def attend_forward(joined, mask, attended, probs_ref, width, score_scale):
    pending = {}
    for h in range(H):
        start, size, high, keep = head_window(width, h)
        q = joined[:, start : start + size] * keep
        k = joined[:, width + start : width + start + size]
        v = joined[:, 2 * width + start : 2 * width + start + size] * keep
        scores = dot(q, k, NT) * score_scale + mask
        exponent = jnp.exp(scores - jnp.max(scores, axis=-1, keepdims=True))
        probs = exponent * (1.0 / jnp.sum(exponent, axis=-1, keepdims=True))
        probs_ref[h] = probs
        result = dot(probs.astype(jnp.bfloat16), v)
        put_head(pending, result, start, size, high, attended, 0)


def attend_backward(joined, head_grad, probs_ref, qkv_grad, width, score_scale):
    pending = [{}, {}, {}]
    for h in range(H):
        start, size, high, keep = head_window(width, h)
        q = joined[:, start : start + size] * keep
        k = joined[:, width + start : width + start + size] * keep
        v = joined[:, 2 * width + start : 2 * width + start + size]
        g = head_grad[:, start : start + size] * keep
        probs = probs_ref[h]
        prob_grad = dot(g, v, NT)
        inner = jnp.sum(probs * prob_grad, axis=-1, keepdims=True)
        score_grad = (probs * (prob_grad - inner) * score_scale).astype(jnp.bfloat16)
        results = (
            dot(score_grad, k),
            dot(score_grad, q, TN),
            dot(probs.astype(jnp.bfloat16), g, TN),
        )
        for which, result in enumerate(results):
            put_head(pending[which], result, start, size, high, qkv_grad, which * width)


def fold_of(row_block, column_block):
    rest = column_block % LANES
    fits = [f for f in range(1, LANES // max(rest, 1) + 1) if row_block % (f * SUBLANES) == 0]
    return column_block // LANES, rest, fits[-1] if fits else 1


def folded_rows(row_block, column_block):
    full, rest, fold = fold_of(row_block, column_block)
    return full * row_block + (row_block // fold if rest else 0)


def fold_piece(value):
    full, rest, fold = fold_of(*value.shape)
    tiles = [value[:, t * LANES : (t + 1) * LANES] for t in range(full)]
    if rest:
        size = value.shape[0] // fold
        parts = [value[f * size : (f + 1) * size, full * LANES :] for f in range(fold)]
        if rest * fold < LANES:
            parts.append(jnp.zeros((size, LANES - rest * fold), value.dtype))
        tiles.append(jnp.concatenate(parts, axis=1))
    return tiles


def unfold_piece(value, target):
    row_block, column_block = target.shape
    full, rest, fold = fold_of(row_block, column_block)
    for t in range(full):
        target[:, t * LANES : (t + 1) * LANES] = value[t * row_block : (t + 1) * row_block]
    if rest:
        size = row_block // fold
        tail = value[full * row_block :]
        for f in range(fold):
            target[f * size : (f + 1) * size, full * LANES :] = tail[:, f * rest : (f + 1) * rest]


def exchange_kernel(
    score_scale,
    seq_size,
    dp_size,
    tokens_ref,
    d_out_ref,
    count_ref,
    order_ref,
    w_qkv_hbm,
    w_out_hbm,
    d_tokens_ref,
    final_ref,
    w_qkv_ref,
    w_out_ref,
    got_tokens,
    got_d_out,
    results,
    joined,
    head_grad,
    attended,
    qkv_grad,
    grad,
    probs_ref,
    live_ref,
    mask_ref,
    pair_sent,
    pair_got,
    dp_sent,
    dp_got,
    held,
    chip_sent,
    chip_got,
    weight_sems,
    tokens_send,
    tokens_recv,
    d_out_send,
    d_out_recv,
    back_send,
    back_recv,
    pair_sems,
    dp_send,
    dp_recv,
    chip_send,
    chip_recv,
):
    rows, width = attended.shape
    steps, slot_count, group, _ = got_tokens.shape
    slots = tokens_ref.shape[0]
    stripe = steps * group
    chips = seq_size // 2
    row_block, column_block = final_ref.shape
    me = lax.axis_index("seq")
    my_dp = lax.axis_index("dp")
    core = lax.rem(me, 2)
    chip = me // 2
    half = seq_size // 2
    far = tuple(reversed(range(half, seq_size)))
    near = tuple(reversed(range(1, half)))
    outer, inner = far[: half // 2], far[half // 2 :]
    staggered = tuple(
        first + core * (second - first) for first, second in zip(far + near, outer + near + inner)
    )

    def peer(k):
        return me ^ k

    def dp_peer(k):
        return lax.rem(my_dp + k, dp_size)

    barrier = pltpu.get_barrier_semaphore()
    for k in range(1, seq_size):
        pl.semaphore_signal(
            barrier,
            inc=1,
            device_id={"seq": peer(k)},
            device_id_type=pl.DeviceIdType.MESH,
        )
    for k in range(1, dp_size):
        pl.semaphore_signal(
            barrier,
            inc=1,
            device_id={"dp": dp_peer(k)},
            device_id_type=pl.DeviceIdType.MESH,
        )
    pl.semaphore_wait(barrier, seq_size - 1 + dp_size - 1)

    def remote(source, target, send, recv, device):
        return pltpu.make_async_remote_copy(
            src_ref=source,
            dst_ref=target,
            send_sem=send,
            recv_sem=recv,
            device_id=device,
            device_id_type=pl.DeviceIdType.MESH,
        )

    def home(ref, owner, g):
        return ref.at[:, pl.ds(pl.multiple_of(owner * stripe + g * group, group), group), :]

    def away(ref, owner, g):
        return ref.at[g, pl.ds(owner * slots, slots)]

    def spread(source, target, send, recv, g, k):
        return remote(
            home(source, peer(k), g),
            away(target, me, g),
            send.at[g, k],
            recv.at[g, k],
            {"seq": peer(k)},
        )

    def keep_own(source, target, recv, g):
        return pltpu.make_async_copy(home(source, me, g), away(target, me, g), recv.at[g, 0])

    def back(g, k):
        return remote(
            away(results, peer(k), g),
            home(d_tokens_ref, me, g),
            back_send.at[g, k],
            back_recv.at[g, k],
            {"seq": peer(k)},
        )

    def back_own(g):
        return pltpu.make_async_copy(
            away(results, me, g), home(d_tokens_ref, me, g), back_recv.at[g, 0]
        )

    moved = (
        (tokens_ref, got_tokens, tokens_send, tokens_recv),
        (d_out_ref, got_d_out, d_out_send, d_out_recv),
    )

    def depart(which, g):
        source, target, send, recv = moved[which]
        for k in staggered:
            spread(source, target, send, recv, g, k).start()
        keep_own(source, target, recv, g).start()

    def arrived(which, g):
        source, target, send, recv = moved[which]
        for k in range(1, seq_size):
            spread(source, target, send, recv, g, k).wait_recv()
        keep_own(source, target, recv, g).wait()

    def give_back(g):
        for k in staggered:
            back(g, k).start()
        back_own(g).start()

    for at in range(min(AHEAD, 2 * steps)):
        depart(at % 2, at // 2)
    weights = (
        pltpu.make_async_copy(w_qkv_hbm, w_qkv_ref, weight_sems.at[0]),
        pltpu.make_async_copy(w_out_hbm, w_out_ref, weight_sems.at[1]),
    )
    for copy in weights:
        copy.start()
    live_ref[...], mask_ref[...] = mask_in_kernel(group, order_ref[...], count_ref[0])
    grad[...] = jnp.zeros_like(grad)
    for copy in weights:
        copy.wait()

    def depart_next(which, g):
        at = AHEAD + which
        later = g + at // 2

        @pl.when(later < steps)
        def _():
            depart(at % 2, later)

    def pair_copy():
        return remote(
            pair_sent, pair_got, pair_sems.at[0], pair_sems.at[1], {"seq": chip * 2 + 1 - core}
        )

    def row_piece(at, parity):
        start = pl.multiple_of((at * 2 + parity) * row_block, row_block)
        return grad[pl.ds(start, row_block), :]

    def pieces_of(value, d):
        start = 0
        for tile in fold_piece(value[:, d * column_block : (d + 1) * column_block]):
            yield slice(start, start + tile.shape[0]), tile
            start += tile.shape[0]

    def dp_copy(k):
        return remote(
            dp_sent.at[dp_peer(k)],
            dp_got.at[k - 1],
            dp_send.at[k - 1],
            dp_recv.at[k - 1],
            {"dp": dp_peer(k)},
        )

    @pl.loop(0, steps)
    def _(g):
        arrived(0, g)
        depart_next(0, g)

        @pl.when(g == steps - 1)
        def _():
            for earlier in range(max(steps - 3, 0)):
                give_back(earlier)

        values = got_tokens[g].astype(jnp.float32).reshape(rows, width)
        center = values - jnp.mean(values, axis=-1, keepdims=True)
        inverse = lax.rsqrt(jnp.mean(center * center, axis=-1, keepdims=True) + 1e-06)
        normalized = center * inverse
        joined[...] = dot(normalized.astype(jnp.bfloat16), w_qkv_ref[...]).astype(jnp.bfloat16)
        attend_forward(joined, mask_ref[...], attended, probs_ref, width, score_scale)

        arrived(1, g)
        depart_next(1, g)
        masked_wide = got_d_out[g].astype(jnp.float32).reshape(rows, width) * live_ref[...]
        masked = masked_wide.astype(jnp.bfloat16)
        grad[...] += dot(attended[...], masked, TN)

        @pl.when(g == steps - 1)
        def _():
            @pl.loop(0, chips)
            def _(at):
                value = row_piece(at, 1 - core)
                for d in range(dp_size):
                    for where, tile in pieces_of(value, d):
                        pair_sent[d, at, where] = tile.astype(jnp.bfloat16)

            pair_copy().start()

        head_grad[...] = dot(masked, w_out_ref[...], NT).astype(jnp.bfloat16)

        @pl.when(g == steps - 1)
        def _():
            pair_copy().wait_recv()

            @pl.loop(0, chips)
            def _(at):
                value = row_piece(at, core)
                for d in range(dp_size):
                    for where, tile in pieces_of(value, d):
                        total = tile + pair_got[d, at, where].astype(jnp.float32)
                        dp_sent[d, at, where] = total.astype(jnp.bfloat16)

            for k in range(1, dp_size):
                dp_copy(k).start()

            for earlier in range(max(steps - 3, 0), steps - 1):
                give_back(earlier)

        attend_backward(joined, head_grad, probs_ref, qkv_grad, width, score_scale)
        normed_grad = dot(qkv_grad[...], w_qkv_ref[...], NT)
        mean_grad = jnp.mean(normed_grad, axis=-1, keepdims=True)
        mean_cross = jnp.mean(normed_grad * normalized, axis=-1, keepdims=True)
        result = masked_wide + inverse * (normed_grad - mean_grad - normalized * mean_cross)
        results[g] = result.reshape(slot_count, group, width).astype(jnp.bfloat16)

    for k in range(1, dp_size):
        dp_copy(k).wait_recv()

    @pl.loop(0, chips)
    def _(at):
        total = dp_sent[my_dp, at].astype(jnp.float32)
        for k in range(1, dp_size):
            total = total + dp_got[k - 1, at].astype(jnp.float32)
        held[at] = total

    def chip_copy(level):
        return remote(
            chip_sent.at[pl.ds(chips - 2 * (chips >> (level + 1)), chips >> (level + 1))],
            chip_got.at[pl.ds(chips - 2 * (chips >> (level + 1)), chips >> (level + 1))],
            chip_send.at[level],
            chip_recv.at[level],
            {"seq": (chip ^ (1 << level)) * 2 + core},
        )

    for level in range(chips.bit_length() - 1):
        left = chips >> (level + 1)
        base = chips - 2 * left
        bit = lax.rem(chip // (1 << level), 2)
        for at in range(left):
            chip_sent[base + at] = held[2 * at + 1 - bit].astype(jnp.bfloat16)
        chip_copy(level).start()
        if level == 0:
            give_back(steps - 1)
        chip_copy(level).wait_recv()
        for at in range(left):
            held[at] = held[2 * at + bit] + chip_got[base + at].astype(jnp.float32)
    unfold_piece(held[0], final_ref)

    pair_copy().wait_send()
    for k in range(1, dp_size):
        dp_copy(k).wait_send()
    for level in range(chips.bit_length() - 1):
        chip_copy(level).wait_send()

    @pl.loop(0, steps)
    def _(g):
        for source, target, send, recv in moved:
            for k in range(1, seq_size):
                spread(source, target, send, recv, g, k).wait_send()
        for k in range(1, seq_size):
            back(g, k).wait()
        back_own(g).wait()


def exchange_part(tokens, d_out, frames, frame_order, w_qkv, w_out, slots, seq_size, dp_size):
    row_count, width = tokens.shape
    slot_count = frame_order.shape[1]
    stripe = row_count // slot_count
    steps = stripe // GROUP
    rows = slot_count * GROUP
    chips = seq_size // 2
    levels = chips.bit_length() - 1
    tokens = tokens.reshape(slots, row_count // slots, width)
    d_out = d_out.reshape(tokens.shape)
    any_space = pl.BlockSpec(memory_space=pl.ANY)
    vmem = pl.BlockSpec(memory_space=pltpu.VMEM)
    smem = pl.BlockSpec(memory_space=pltpu.SMEM)
    narrow = jnp.bfloat16
    share = (width // seq_size, width // dp_size)
    parts = (chips, folded_rows(*share), LANES)
    crossing = pltpu.SemaphoreType.DMA((steps, seq_size))
    d_tokens, final = pl.pallas_call(
        functools.partial(exchange_kernel, 1.0 / math.sqrt(width // H), seq_size, dp_size),
        in_specs=[any_space, any_space, smem, vmem, any_space, any_space],
        out_specs=[any_space, vmem],
        out_shape=[
            jax.ShapeDtypeStruct(tokens.shape, narrow),
            jax.ShapeDtypeStruct(share, jnp.float32),
        ],
        scratch_shapes=[
            pltpu.VMEM(w_qkv.shape, narrow),
            pltpu.VMEM(w_out.shape, narrow),
            pltpu.VMEM((steps, slot_count, GROUP, width), narrow),
            pltpu.VMEM((steps, slot_count, GROUP, width), narrow),
            pltpu.VMEM((steps, slot_count, GROUP, width), narrow),
            pltpu.VMEM((rows, 3 * width), narrow),
            pltpu.VMEM((rows, width), narrow),
            pltpu.VMEM((rows, width), narrow),
            pltpu.VMEM((rows, 3 * width), narrow),
            pltpu.VMEM((width, width), jnp.float32),
            pltpu.VMEM((H, rows, rows), jnp.float32),
            pltpu.VMEM((rows, 1), jnp.float32),
            pltpu.VMEM((rows, rows), jnp.float32),
            pltpu.VMEM((dp_size, *parts), narrow),
            pltpu.VMEM((dp_size, *parts), narrow),
            pltpu.VMEM((dp_size, *parts), narrow),
            pltpu.VMEM((dp_size - 1, *parts), narrow),
            pltpu.VMEM(parts, jnp.float32),
            pltpu.VMEM((chips - 1, *parts[1:]), narrow),
            pltpu.VMEM((chips - 1, *parts[1:]), narrow),
            pltpu.SemaphoreType.DMA((2,)),
            crossing,
            crossing,
            crossing,
            crossing,
            crossing,
            crossing,
            pltpu.SemaphoreType.DMA((2,)),
            pltpu.SemaphoreType.DMA((dp_size - 1,)),
            pltpu.SemaphoreType.DMA((dp_size - 1,)),
            pltpu.SemaphoreType.DMA((levels,)),
            pltpu.SemaphoreType.DMA((levels,)),
        ],
        compiler_params=pltpu.CompilerParams(
            collective_id=0, has_side_effects=True, vmem_limit_bytes=VMEM_BYTES
        ),
    )(tokens, d_out, frames, frame_order, w_qkv, w_out)
    return d_tokens, final


def body(tokens, d_out, frames, frame_order, w_qkv, w_out):
    _, row_count, width = tokens.shape
    seq_size = lax.axis_size("seq")
    slot_count = frame_order.shape[1]
    stripe = row_count // slot_count
    patch_count = row_count * seq_size // slot_count
    slots = max(1, row_count // patch_count)
    piece = row_count // slots // seq_size
    live_slots = (frame_order[0] < frames[0]).astype(jnp.float32)

    dp_size = lax.axis_size("dp")
    if (
        piece == stripe
        and stripe % GROUP == 0
        and seq_size & (seq_size - 1) == 0
        and seq_size > 2
        and dp_size > 1
        and width % (16 * seq_size) == 0
    ):
        d_rows, final_out = exchange_part(
            tokens[0], d_out[0], frames, frame_order, w_qkv, w_out, slots, seq_size, dp_size
        )
        return (d_rows.reshape(tokens.shape), final_out)

    def spread(rows):
        sent = rows.reshape(slots, seq_size, piece, width)
        got = lax.all_to_all(sent, "seq", split_axis=1, concat_axis=0, tiled=True)
        return got.reshape(slot_count, stripe, width)

    d_rows, grad_out = local_part(spread(tokens), spread(d_out), live_slots, w_qkv, w_out)
    back = d_rows.reshape(seq_size * slots, 1, piece, width)
    d_tokens = lax.all_to_all(back, "seq", split_axis=0, concat_axis=1, tiled=True)
    share = lax.psum_scatter(
        grad_out.astype(jnp.bfloat16), "dp", scatter_dimension=1, tiled=True
    ).astype(jnp.float32)
    final_out = lax.psum_scatter(share, "seq", scatter_dimension=0, tiled=True)
    return (d_tokens.reshape(tokens.shape), final_out)


def solution(mesh):
    placed = (P("dp", "seq", None), P("dp", "seq", None), P("dp"), P("dp", None), P(), P())
    return jax.shard_map(
        body,
        mesh=mesh,
        in_specs=placed,
        out_specs=(P("dp", "seq", None), P("seq", "dp")),
        check_vma=False,
    )
```
